256 devices in a mesh: chain: 4 (over z_lo, core), mesh: 16 (over z_hi, y), probe: 4 (over x).
Axes of the slice: x: 4, y: 4, z: 8 (z_hi: 4, z_lo: 2; z = z_hi * 2 + z_lo), core: 2. Of those that a mesh axis runs over, the one named last changes fastest.
Arguments:
- signs: int32 [256, 8, 4096], P('probe', 'chain', 'mesh'), may hold values from 0 to 1
- border_signs: int32 [256, 512], P('probe'), may hold values from 0 to 1
- inverse_factors: bfloat16 [8, 4096, 4096], P('chain', 'mesh'), may hold values from -2 to 2, as said below
- couplings: bfloat16 [8, 32, 4, 128, 128], P('chain', 'mesh'), may hold values from -0.15625 to 0.15625
- coupling_cols: int32 [8, 32, 4], P('chain', 'mesh'), may hold values from 0 to 31, all different within a row
- border_rows: bfloat16 [8, 512, 4096], P('chain', None, 'mesh'), may hold values from -0.046875 to 0.046875
- border_inverse: bfloat16 [512, 512], replicated, may hold values from -2 to 2, as said below
Outputs:
- solved: bfloat16 [256, 8, 4096], P('probe', 'chain', 'mesh')
- border_solved: float32 [256, 512], P('probe')
- node_var: float32 [8, 4096], P('chain', 'mesh')
- border_var: float32 [512], replicated
The draws below stay inside these ranges and needn't reach their ends.
Inputs may be any that keep to these rules, and one draw needn't show every extreme that they name: `inverse_factors`: lower triangular; diagonal entries between 0.5 and 2. `border_inverse`: lower triangular; diagonal entries between 0.5 and 2. `coupling_cols`: the 4 block columns of one block row differ.
All inputs are finite; a program needn't handle non-finite values.
Results may differ from the reference program's by a relative error of at most 0.015.
Values may be sent and summed in bfloat16 or wider, within the bound.
No kernel may reach another device: no remote copies, remote signals or barrier semaphores. Data moves between devices by JAX's collectives and lax.ppermute only.
A program may use at most 64 MiB of HBM per device.

```python
import math
import jax
import jax.numpy as jnp
from jax import lax

B = 4096
BLK = 128
K = 4
F = 512
NBR = 32
TT = 8
PROBES = 256


def lower_inverse(key, lead, order):
    first, second = jax.random.split(key)
    rows = jnp.arange(order)[:, None]
    cols = jnp.arange(order)[None, :]
    spread = jnp.clip(jax.random.normal(first, (lead, order, order), jnp.float32), -6.0, 6.0)
    lower = jnp.where(cols < rows, spread * (0.6 / math.sqrt(order)), 0.0)
    diagonal = jnp.exp(jax.random.uniform(second, (lead, order, 1), jnp.float32, math.log(0.5), math.log(2.0)))
    return lower + jnp.where(cols == rows, diagonal, 0.0)


def draw_inverse_factors(key, part):
    return lower_inverse(key, TT, B).astype(jnp.bfloat16)


def draw_border_inverse(key, part):
    return lower_inverse(jax.random.fold_in(key, 7), 1, F)[0].astype(jnp.bfloat16)


def plant(array, own_key, smallest, largest):
    index_at = [jax.random.randint(jax.random.fold_in(own_key, axis), (), 0, length) for axis, length in enumerate(array.shape)]
    longest = array.shape.index(max(array.shape))
    next_to = index_at[:longest] + [(index_at[longest] + 1) % array.shape[longest]] + index_at[longest + 1:]
    return array.at[tuple(index_at)].set(smallest).at[tuple(next_to)].set(largest)


def steps_of(own_key, dims, pieces, low, high):
    factor_of = 1.0
    for dim, parts in pieces:
        steps = jax.random.uniform(jax.random.fold_in(jax.random.fold_in(own_key, 6), dim), (parts,), jnp.float32, low / len(pieces), high / len(pieces))
        factor_of = factor_of * jnp.repeat(jnp.exp(steps), dims[dim] // parts).reshape((-1,) + (1,) * (len(dims) - 1 - dim))
    return factor_of


def distinct(stream_key, rows, number_of, top, lift):
    order = jax.random.permutation(jax.random.fold_in(stream_key, 1), number_of)
    favour = order
    for power in range(3):
        favour = favour * favour // number_of
    favour = favour * lift // number_of
    tickets = jax.random.randint(jax.random.fold_in(stream_key, 2), (rows, number_of), 0, 4096) + favour
    fixed_rows = jax.random.permutation(jax.random.fold_in(stream_key, 3), rows)[jnp.arange(number_of) % rows]
    tickets = jnp.where(jnp.arange(rows)[:, None] == fixed_rows[None, :], 1 << 14, tickets)
    merit = tickets * number_of + jnp.arange(number_of)
    return lax.top_k(merit.astype(jnp.int32), top)[1].astype(jnp.int32)


def centred(stream_key, shape, scale, reach, pieces=(), kind=jnp.bfloat16):
    values = scale * jax.random.normal(stream_key, shape, jnp.float32)
    if pieces:
        values = values * steps_of(stream_key, shape, pieces, -0.22, 0.18)
    return jnp.clip(values, -reach, reach).astype(kind)


def setup_inputs(seed: int = 0) -> dict:
    arg_keys = jax.random.split(jax.random.key(seed), 8)
    signs = plant(jax.random.randint(arg_keys[0], (PROBES, TT, B), 0, 2), jax.random.fold_in(arg_keys[0], 1), 0, 1).astype(jnp.int32)
    border_signs = plant(jax.random.randint(arg_keys[1], (PROBES, F), 0, 2), jax.random.fold_in(arg_keys[1], 1), 0, 1).astype(jnp.int32)
    inverse_factors = draw_inverse_factors(jax.random.fold_in(arg_keys[7], 71), 0)
    couplings = centred(arg_keys[3], (TT, NBR, K, BLK, BLK), (3 * K * BLK) ** -0.5, 0.15625, ((0, 4), (1, 16)))
    coupling_cols = distinct(arg_keys[4], TT * NBR, NBR, K, 0).reshape((TT, NBR, K))
    border_rows = centred(arg_keys[5], (TT, F, B), (TT * B // 2) ** -0.5, 0.046875, ((0, 4), (2, 16)))
    border_inverse = draw_border_inverse(jax.random.fold_in(arg_keys[7], 71), 0)
    return {"signs": signs, "border_signs": border_signs, "inverse_factors": inverse_factors, "couplings": couplings, "coupling_cols": coupling_cols, "border_rows": border_rows, "border_inverse": border_inverse}


def reference(signs, border_signs, inverse_factors, couplings, coupling_cols, border_rows, border_inverse):
    source = (2 * signs - 1).astype(jnp.float32)
    border_source = (2 * border_signs - 1).astype(jnp.float32)
    count = source.shape[0]
    width = source.shape[2]
    prev = jnp.zeros((count, width), jnp.bfloat16)
    outputs = []
    coupled_border = jnp.zeros((count, border_rows.shape[1]), jnp.float32)
    for step in range(TT):
        blocks = prev.reshape(count, NBR, BLK)[:, coupling_cols[step]]
        coupled = jnp.einsum("prkc,rkdc->prd", blocks.astype(jnp.float32), couplings[step].astype(jnp.float32)).reshape(count, width)
        resid_b = (source[:, step] - coupled).astype(jnp.bfloat16)
        solved_now = jnp.dot(resid_b, inverse_factors[step].T, preferred_element_type=jnp.float32).astype(jnp.bfloat16)
        outputs.append(solved_now)
        coupled_border = coupled_border + jnp.dot(solved_now, border_rows[step].T, preferred_element_type=jnp.float32)
        prev = solved_now
    solved = jnp.stack(outputs, axis=1)
    border_resid = (border_source - coupled_border).astype(jnp.bfloat16)
    border_solved = jnp.dot(border_resid, border_inverse.T, preferred_element_type=jnp.float32)
    node_var = jnp.mean(jnp.square(solved.astype(jnp.float32)), axis=0)
    border_var = jnp.mean(jnp.square(border_solved), axis=0)
    return solved, border_solved, node_var, border_var
```

```python
import functools

import jax
import jax.numpy as jnp
from jax import lax
from jax.experimental import pallas as pl
from jax.experimental.pallas import tpu as pltpu
from jax.sharding import Mesh, PartitionSpec as P

AXES = ("zl", "core", "zh", "y", "x")
CHAIN, NODES = ("zl", "core"), ("zh", "y")
NT = (((1,), (1,)), ((), ()))
CHUNKS = 4


def couple_kernel(cols, who, x_ref, own_c, other_c, s_ref, out_ref, c_buf, sem, *, step):
    rows, slots, block = c_buf.shape[0], c_buf.shape[1], c_buf.shape[2]
    mine = pltpu.make_async_copy(own_c.at[step % 2], c_buf, sem)
    theirs = pltpu.make_async_copy(other_c.at[step % 2], c_buf, sem)

    @pl.when(who[0] == step // 2)
    def _():
        mine.start()

    @pl.when(who[0] != step // 2)
    def _():
        theirs.start()

    mine.wait()
    per = x_ref.shape[2] // block
    for row in range(rows):
        total = None
        for slot in range(slots):
            col = cols[(step * rows + row) * slots + slot]
            lanes = pl.ds(pl.multiple_of((col % per) * block, block), block)
            term = lax.dot_general(
                x_ref[col // per, :, lanes], c_buf[row, slot], NT, preferred_element_type=jnp.float32
            )
            total = term if total is None else total + term
        span = slice(row * block, (row + 1) * block)
        resid = (s_ref[:, span] - total).astype(jnp.bfloat16)
        for peer in range(out_ref.shape[0]):
            out_ref[peer, :, span] = resid


def apply_kernel(who, r_ref, own_l, other_l, out_ref, spread_ref, l_buf, sems, *, step):
    width = l_buf.shape[2]

    def copies(source):
        return [
            pltpu.make_async_copy(
                source.at[step % 2, :, pl.ds(i * width, width)], l_buf.at[i], sems.at[i]
            )
            for i in range(CHUNKS)
        ]

    mine, theirs = copies(own_l), copies(other_l)

    @pl.when(who[0] == step // 2)
    def _():
        for copy in mine:
            copy.start()

    @pl.when(who[0] != step // 2)
    def _():
        for copy in theirs:
            copy.start()

    peers, _, piece = r_ref.shape
    total = None
    for i in range(CHUNKS):
        mine[i].wait()
        per = peers // CHUNKS
        left = jnp.concatenate([r_ref[i * per + p] for p in range(per)], axis=1)
        term = lax.dot_general(left, l_buf[i], NT, preferred_element_type=jnp.float32)
        total = term if total is None else total + term
    result = total.astype(jnp.bfloat16)
    out_ref[...] = result
    if spread_ref is not None:
        for peer in range(peers):
            spread_ref[peer] = result


def vmem():
    return pl.BlockSpec(memory_space=pltpu.VMEM)


def smem():
    return pl.BlockSpec(memory_space=pltpu.SMEM)


def hbm():
    return pl.BlockSpec(memory_space=pl.ANY)


def couple(cols, who, pieces, own_c, other_c, source, step):
    peers, probes, piece = pieces.shape
    return pl.pallas_call(
        functools.partial(couple_kernel, step=step),
        out_shape=jax.ShapeDtypeStruct((peers, probes, piece), jnp.bfloat16),
        in_specs=[smem(), smem(), vmem(), hbm(), hbm(), vmem()],
        out_specs=vmem(),
        scratch_shapes=[pltpu.VMEM(own_c.shape[1:], own_c.dtype), pltpu.SemaphoreType.DMA],
        name=f"couple{step}",
    )(cols, who, pieces, own_c, other_c, source)


def apply_factor(who, pieces, own_l, other_l, step):
    peers, probes, piece = pieces.shape
    rows, width = own_l.shape[1:]
    return pl.pallas_call(
        functools.partial(apply_kernel, step=step),
        out_shape=(
            jax.ShapeDtypeStruct((probes, rows), jnp.bfloat16),
            jax.ShapeDtypeStruct((peers, probes, rows), jnp.bfloat16),
        ),
        in_specs=[smem(), vmem(), hbm(), hbm()],
        out_specs=(vmem(), vmem()),
        scratch_shapes=[
            pltpu.VMEM((CHUNKS, rows, width // CHUNKS), own_l.dtype),
            pltpu.SemaphoreType.DMA((CHUNKS,)),
        ],
        compiler_params=pltpu.CompilerParams(vmem_limit_bytes=24 << 20),
        name=f"apply{step}",
    )(who, pieces, own_l, other_l)


def exchange(spread):
    return lax.all_to_all(spread, NODES, 0, 0)


def shards(
    signs, border_signs, inverse_factors, couplings, coupling_cols, border_rows, border_inverse
):
    local_probes, own_steps, local = signs.shape
    cores = lax.axis_size("core")
    peers = lax.axis_size("zh") * lax.axis_size("y")
    probes = local_probes // cores
    steps = own_steps * cores
    core = lax.axis_index("core")
    first = core == 0
    who = jnp.reshape(core, (1,)).astype(jnp.int32)

    def swap(value):
        return lax.ppermute(value, "core", [(0, 1), (1, 0)])

    def in_order(own, other):
        return jnp.concatenate([jnp.where(first, own, other), jnp.where(first, other, own)], axis=0)

    source = (2 * signs - 1).astype(jnp.bfloat16).reshape(cores, probes, own_steps, local)
    source = source.transpose(0, 2, 1, 3)
    own_source = jnp.where(first, source[0], source[1])
    other_source = swap(jnp.where(first, source[1], source[0]))
    source4 = in_order(own_source, other_source)
    other_l = swap(inverse_factors)
    other_c = swap(couplings)
    cols = in_order(coupling_cols, swap(coupling_cols)).reshape(-1)
    source_f32 = source4.astype(jnp.float32)

    pieces = None
    for turn in range(lax.axis_size("zl")):
        results = []
        for step in range(steps):
            if pieces is None:
                spread = jnp.broadcast_to(source4[step][None], (peers, probes, local))
            else:
                spread = couple(cols, who, pieces, couplings, other_c, source_f32[step], step)
            now, spread_now = apply_factor(who, exchange(spread), inverse_factors, other_l, step)
            results.append(now)
            if step + 1 < steps:
                pieces = exchange(spread_now)
        if turn + 1 < lax.axis_size("zl"):
            moved = lax.ppermute(now, "zl", [(turn, turn + 1)])
            pieces = exchange(jnp.broadcast_to(moved[None], (peers, probes, local)))

    solved4 = jnp.stack(results)
    mine = jnp.where(first, solved4[:own_steps], solved4[own_steps:])
    theirs = swap(jnp.where(first, solved4[own_steps:], solved4[:own_steps]))
    solved = jnp.concatenate([jnp.where(first, mine, theirs), jnp.where(first, theirs, mine)], axis=1)
    solved = solved.transpose(1, 0, 2)

    rows4 = in_order(border_rows, swap(border_rows))
    partial = jnp.zeros((probes, border_rows.shape[1]), jnp.float32)
    for step in range(steps):
        partial = partial + lax.dot_general(results[step], rows4[step], NT, preferred_element_type=jnp.float32)
    group = ("zl",) + NODES
    members = lax.axis_size("zl") * peers
    share = probes // members
    parts = lax.all_to_all(partial.reshape(members, share, -1), group, 0, 0)
    coupled_border = jnp.sum(parts, axis=0)
    at = core * probes + lax.axis_index(group) * share
    border_source = (2 * lax.dynamic_slice_in_dim(border_signs, at, share, 0) - 1).astype(jnp.float32)
    border_resid = (border_source - coupled_border).astype(jnp.bfloat16)
    border_part = lax.dot_general(border_resid, border_inverse, NT, preferred_element_type=jnp.float32)
    whole = CHAIN + NODES
    spread = jnp.broadcast_to(border_part[None], (members * cores,) + border_part.shape)
    gathered = lax.all_to_all(spread, whole, 0, 0)
    gathered = gathered.reshape(lax.axis_size("zl"), cores, peers * share, -1).transpose(1, 0, 2, 3)
    border_solved = gathered.reshape(local_probes, -1)

    total_probes = local_probes * lax.axis_size("x")
    node_sums = jnp.sum(jnp.square(solved.astype(jnp.float32)), axis=0)
    border_sums = jnp.sum(jnp.square(border_solved), axis=0)
    node_sums, border_sums = lax.psum((node_sums, border_sums), "x")
    return solved, border_solved, node_sums / total_probes, border_sums / total_probes


def solution(mesh):
    sizes = mesh.shape
    devices = mesh.devices.reshape(2, sizes["chain"] // 2, 4, sizes["mesh"] // 4, sizes["probe"])
    return jax.shard_map(
        shards,
        mesh=Mesh(devices, AXES),
        in_specs=(
            P("x", CHAIN, NODES),
            P("x", None),
            P(CHAIN, NODES, None),
            P(CHAIN, NODES, None, None, None),
            P(CHAIN, NODES, None),
            P(CHAIN, None, NODES),
            P(),
        ),
        out_specs=(P("x", CHAIN, NODES), P("x", None), P(CHAIN, NODES), P()),
        check_vma=False,
    )
```

```python
import functools

import jax
import jax.numpy as jnp
from jax import lax
from jax.experimental import pallas as pl
from jax.experimental.pallas import tpu as pltpu
from jax.sharding import Mesh, PartitionSpec as P

AXES = ("zl", "core", "zh", "y", "x")
CHAIN, NODES = ("zl", "core"), ("zh", "y")
NT = (((1,), (1,)), ((), ()))


def start_one_of(use_first, first, second):
    @pl.when(use_first)
    def _():
        for copy in first:
            copy.start()

    @pl.when(jnp.logical_not(use_first))
    def _():
        for copy in second:
            copy.start()


def couple_kernel(cols, place, x_ref, s_ref, *refs, step, lines, per_core):
    own_c, other_c = refs[:lines], refs[lines : 2 * lines]
    out_ref, c_buf, sems = refs[2 * lines :]
    _, rows, slots, block, _ = c_buf.shape
    own, other = (
        [pltpu.make_async_copy(c[k].at[step % per_core], c_buf.at[k], sems.at[k]) for k in range(lines)]
        for c in (own_c, other_c)
    )
    start_one_of(place[0] == step // per_core, own, other)
    per = x_ref.shape[2] // block
    probes = x_ref.shape[1]
    for k in range(lines):
        own[k].wait()
        home = lax.rem(place[1] + lines - k, lines) * rows
        for row in range(rows):
            total = None
            for slot in range(0, slots, 2):
                left = []
                for pair in range(2):
                    col = cols[k, (step * rows + row) * slots + slot + pair]
                    lanes = pl.ds(pl.multiple_of((col % per) * block, block), block)
                    left.append(x_ref[col // per, :, lanes])
                term = lax.dot_general(
                    jnp.concatenate(left, axis=1),
                    jnp.concatenate([c_buf[k, row, slot], c_buf[k, row, slot + 1]], axis=1),
                    NT,
                    preferred_element_type=jnp.float32,
                )
                total = term if total is None else total + term
            span = slice(row * block, (row + 1) * block)
            source = s_ref[k, step * probes : (step + 1) * probes, span].astype(jnp.float32)
            lanes = pl.ds(pl.multiple_of((home + row) * block, block), block)
            out_ref[:, lanes] = (source - total).astype(jnp.bfloat16)


def apply_kernel(place, *refs, step, lines, per_core, spread):
    pieces, (own_l, other_l) = refs[:lines], refs[lines : lines + 2]
    outs, (r_buf, l_buf, sems) = refs[lines + 2 : -3], refs[-3:]
    width = l_buf.shape[2]
    own, other = (
        [
            pltpu.make_async_copy(
                source.at[step % per_core, :, pl.ds(i * width, width)], l_buf.at[i], sems.at[i]
            )
            for i in range(l_buf.shape[0])
        ]
        for source in (own_l, other_l)
    )
    start_one_of(place[0] == step // per_core, own, other)
    for k in range(lines):
        r_buf[lax.rem(place[2] + lines - k, lines)] = pieces[k][...]
    rows = l_buf.shape[1]
    total = None
    for i in range(l_buf.shape[0]):
        own[i].wait()
        left = jnp.concatenate([r_buf[y, :, i * rows : (i + 1) * rows] for y in range(lines)], axis=1)
        term = lax.dot_general(left, l_buf[i], NT, preferred_element_type=jnp.float32)
        total = term if total is None else total + term
    result = total.astype(jnp.bfloat16)
    outs[0][...] = result
    if spread:
        for peer in range(outs[1].shape[0]):
            outs[1][peer] = result


VMEM = pl.BlockSpec(memory_space=pltpu.VMEM)
SMEM = pl.BlockSpec(memory_space=pltpu.SMEM)
HBM = pl.BlockSpec(memory_space=pltpu.HBM)
PARAMS = pltpu.CompilerParams(vmem_limit_bytes=12 << 20)


def couple(cols, place, pieces, source, own_c, other_c, step):
    lines = len(own_c)
    per_core, rows, slots, block, _ = own_c[0].shape
    return pl.pallas_call(
        functools.partial(couple_kernel, step=step, lines=lines, per_core=per_core),
        out_shape=jax.ShapeDtypeStruct((pieces.shape[1], lines * rows * block), jnp.bfloat16),
        in_specs=[SMEM, SMEM, VMEM, VMEM] + [HBM] * (2 * lines),
        out_specs=VMEM,
        scratch_shapes=[
            pltpu.VMEM((lines, rows, slots, block, block), jnp.bfloat16),
            pltpu.SemaphoreType.DMA((lines,)),
        ],
        compiler_params=PARAMS,
        name=f"couple{step}",
    )(cols, place, pieces, source, *own_c, *other_c)


def apply_factor(place, pieces, own_l, other_l, step, peers):
    lines = len(pieces)
    probes = pieces[0].shape[0]
    per_core, rows, width = own_l.shape
    shapes = [jax.ShapeDtypeStruct((probes, rows), jnp.bfloat16)]
    if peers:
        shapes.append(jax.ShapeDtypeStruct((peers, probes, rows), jnp.bfloat16))
    return pl.pallas_call(
        functools.partial(apply_kernel, step=step, lines=lines, per_core=per_core, spread=bool(peers)),
        out_shape=tuple(shapes),
        in_specs=[SMEM] + [VMEM] * lines + [HBM] * 2,
        out_specs=tuple([VMEM] * len(shapes)),
        scratch_shapes=[
            pltpu.VMEM((lines,) + pieces[0].shape, jnp.bfloat16),
            pltpu.VMEM((lines, rows, width // lines), own_l.dtype),
            pltpu.SemaphoreType.DMA((lines,)),
        ],
        compiler_params=PARAMS,
        name=f"apply{step}",
    )(place, *pieces, own_l, other_l)


def line(value, axis):
    size = lax.axis_size(axis)
    moved = {
        k: lax.ppermute(value, axis, [(i, (i + k) % size) for i in range(size)])
        for k in range(1, size)
    }
    return [value] + [moved[k] for k in range(1, size)]


def swap(value):
    return lax.ppermute(value, "core", [(0, 1), (1, 0)])


def shards(
    signs, border_signs, inverse_factors, couplings, coupling_cols, border_rows, border_inverse
):
    local_probes, own_steps, local = signs.shape
    cores, turns = lax.axis_size("core"), lax.axis_size("zl")
    peers = lax.axis_size("zh") * lax.axis_size("y")
    probes = local_probes // cores
    steps = own_steps * cores
    core = lax.axis_index("core")
    first = core == 0
    place = jnp.stack([core, lax.axis_index("zh"), lax.axis_index("y")]).astype(jnp.int32)

    def in_order(own, other):
        return jnp.concatenate([jnp.where(first, own, other), jnp.where(first, other, own)], axis=0)

    source = (2 * signs - 1).astype(jnp.bfloat16).reshape(cores, probes, own_steps, local)
    source = source.transpose(0, 2, 1, 3)
    flat_cols = coupling_cols.reshape(1, -1).astype(jnp.bfloat16)
    tail = jnp.pad(flat_cols, ((0, 15), (0, local - flat_cols.shape[1])))

    def packed(half):
        return jnp.concatenate([half.reshape(own_steps * probes, local), tail], axis=0)

    own_half = packed(jnp.where(first, source[0], source[1]))
    other_half = swap(packed(jnp.where(first, source[1], source[0])))
    low, high = jnp.where(first, own_half, other_half), jnp.where(first, other_half, own_half)
    split = own_steps * probes
    cols = jnp.concatenate([low[split : split + 1, : flat_cols.shape[1]], high[split : split + 1, : flat_cols.shape[1]]], axis=1)
    cols = jnp.pad(cols, ((0, 15), (0, local - cols.shape[1])))
    bundle = jnp.concatenate([low[:split], high[:split], cols], axis=0)
    bundles = line(bundle, "zh")
    bundles, inverse_factors, couplings, border_rows = lax.optimization_barrier(
        (bundles, inverse_factors, couplings, border_rows)
    )
    source = jnp.stack(bundles)
    cols = source[:, steps * probes, : 2 * flat_cols.shape[1]].astype(jnp.int32)
    zh = lax.axis_index("zh")
    lines = len(bundles)
    begin = [bundles[0][:probes]] + [b[:probes] for b in bundles[1:]]
    resid = jnp.zeros((probes, lines * local), jnp.bfloat16)
    for k in range(lines):
        at = ((zh + lines - k) % lines) * local
        resid = lax.dynamic_update_slice(resid, begin[k], (0, at))

    other_l = swap(inverse_factors)
    own_c = line(couplings, "zh")
    other_c = [swap(c) for c in own_c]

    pieces = None
    for turn in range(turns):
        results = []
        for step in range(steps):
            if pieces is not None:
                resid = couple(cols, place, pieces, source, own_c, other_c, step)
            more = step + 1 < steps
            outs = apply_factor(place, line(resid, "y"), inverse_factors, other_l, step, peers if more else 0)
            results.append(outs[0])
            if more:
                pieces = lax.all_to_all(outs[1], NODES, 0, 0)
        if turn + 1 < turns:
            moved = lax.ppermute(outs[0], "zl", [(turn, turn + 1)])
            pieces = lax.all_to_all(jnp.broadcast_to(moved[None], (peers, probes, local)), NODES, 0, 0)

    rows4 = in_order(border_rows, swap(border_rows))
    partial = jnp.zeros((probes, border_rows.shape[1]), jnp.float32)
    for step in range(steps):
        partial = partial + lax.dot_general(results[step], rows4[step], NT, preferred_element_type=jnp.float32)
    for axis in ("y", "zh", "zl"):
        partial = functools.reduce(jnp.add, line(partial, axis))
    halves = border_signs.reshape(cores, probes, -1)
    border_source = (2 * jnp.where(first, halves[0], halves[1]) - 1).astype(jnp.float32)
    border_resid = (border_source - partial).astype(jnp.bfloat16)
    own_border = lax.dot_general(border_resid, border_inverse, NT, preferred_element_type=jnp.float32)
    border_solved = in_order(own_border, swap(own_border))

    solved4 = jnp.stack(results)
    mine = jnp.where(first, solved4[:own_steps], solved4[own_steps:])
    theirs = swap(jnp.where(first, solved4[own_steps:], solved4[:own_steps]))
    solved = jnp.concatenate([jnp.where(first, mine, theirs), jnp.where(first, theirs, mine)], axis=1)
    solved = solved.transpose(1, 0, 2)

    total_probes = local_probes * lax.axis_size("x")
    node_sums = jnp.sum(jnp.square(solved.astype(jnp.float32)), axis=0)
    border_sums = jnp.sum(jnp.square(border_solved), axis=0)
    node_sums, border_sums = lax.psum((node_sums, border_sums), "x")
    return solved, border_solved, node_sums / total_probes, border_sums / total_probes


def solution(mesh):
    sizes = mesh.shape
    devices = mesh.devices.reshape(2, sizes["chain"] // 2, 4, sizes["mesh"] // 4, sizes["probe"])
    return jax.shard_map(
        shards,
        mesh=Mesh(devices, AXES),
        in_specs=(
            P("x", CHAIN, NODES),
            P("x", None),
            P(CHAIN, NODES, None),
            P(CHAIN, NODES, None, None, None),
            P(CHAIN, NODES, None),
            P(CHAIN, None, NODES),
            P(),
        ),
        out_specs=(P("x", CHAIN, NODES), P("x", None), P(CHAIN, NODES), P()),
        check_vma=False,
    )
```

```python
import functools

import jax
import jax.numpy as jnp
from jax import lax
from jax.experimental import pallas as pl
from jax.experimental.pallas import tpu as pltpu
from jax.sharding import Mesh, PartitionSpec as P

AXES = ("zl", "core", "zh", "y", "x")
CHAIN, NODES = ("zl", "core"), ("zh", "y")
NT = (((1,), (1,)), ((), ()))


def start_one_of(use_first, first, second):
    @pl.when(use_first)
    def _():
        for copy in first:
            copy.start()

    @pl.when(jnp.logical_not(use_first))
    def _():
        for copy in second:
            copy.start()


def arrange_kernel(place, own_ref, other_ref, *refs, per_core):
    outs, sems = refs[:-1], refs[-1]

    def copies(source, step):
        return [pltpu.make_async_copy(source(step % per_core), outs[step], sems.at[step])]

    waits = []
    for step in range(len(outs)):
        own, other = copies(own_ref, step), copies(other_ref, step)
        start_one_of(place[0] == step // per_core, own, other)
        waits += own
    for copy in waits:
        copy.wait()


def factor_kernel(place, own_ref, other_ref, *refs, per_core):
    arrange_kernel(place, lambda i: own_ref.at[i], lambda i: other_ref.at[i], *refs, per_core=per_core)


def coupling_kernel(place, own_ref, other_ref, after, *refs, per_core):
    size = refs[0].shape[1]
    arrange_kernel(
        place,
        lambda i: own_ref.at[:, pl.ds(i * size, size)],
        lambda i: other_ref.at[:, pl.ds(i * size, size)],
        *refs,
        per_core=per_core,
    )


def couple_kernel(cols, x_ref, s_ref, c_ref, out_ref, *, step, slots):
    lines, tall, block = c_ref.shape
    rows = tall // (slots * block)
    per = x_ref.shape[2] // block
    probes = x_ref.shape[1]

    def body(k, carry):
        for row in range(rows):
            total = None
            for slot in range(0, slots, 2):
                left, right = [], []
                for pair in range(2):
                    col = cols[k, (step * rows + row) * slots + slot + pair]
                    lanes = pl.ds(pl.multiple_of((col % per) * block, block), block)
                    left.append(x_ref[col // per, :, lanes])
                    at = (row * slots + slot + pair) * block
                    right.append(c_ref[k, at : at + block, :])
                term = lax.dot_general(
                    jnp.concatenate(left, axis=1),
                    jnp.concatenate(right, axis=1),
                    NT,
                    preferred_element_type=jnp.float32,
                )
                total = term if total is None else total + term
            at = (row * s_ref.shape[1]) // rows + step * probes
            source = s_ref[k, at : at + probes, :].astype(jnp.float32)
            lanes = pl.ds(pl.multiple_of((k * rows + row) * block, block), block)
            out_ref[:, lanes] = (source - total).astype(jnp.bfloat16)
        return carry

    lax.fori_loop(0, lines, body, 0)


def finish(total, outs):
    result = total.astype(jnp.bfloat16)
    outs[0][...] = result
    if len(outs) > 1:
        for peer in range(outs[1].shape[0]):
            outs[1][peer] = result


def first_kernel(r_ref, l_ref, *outs):
    width = r_ref.shape[2]

    def body(i, total):
        for j in range(4):
            lanes = pl.ds(pl.multiple_of((i * 4 + j) * width, width), width)
            total = total + lax.dot_general(
                r_ref[i * 4 + j], l_ref[:, lanes], NT, preferred_element_type=jnp.float32
            )
        return total

    start = jnp.zeros((r_ref.shape[1], l_ref.shape[0]), jnp.float32)
    finish(lax.fori_loop(0, r_ref.shape[0] // 4, body, start), outs)


def apply_kernel(place, *refs, lines):
    pieces, l_ref, outs = refs[:lines], refs[lines], refs[lines + 1 :]
    width = l_ref.shape[0]

    def body(zh, total):
        for k in range(lines):
            y = lax.rem(place[2] + lines - k, lines)
            lanes = pl.ds(pl.multiple_of((zh * lines + y) * width, width), width)
            here = pl.ds(pl.multiple_of(zh * width, width), width)
            total = total + lax.dot_general(
                pieces[k][:, here], l_ref[:, lanes], NT, preferred_element_type=jnp.float32
            )
        return total

    start = jnp.zeros((pieces[0].shape[0], width), jnp.float32)
    finish(lax.fori_loop(0, pieces[0].shape[1] // width, body, start), outs)


VMEM = pl.BlockSpec(memory_space=pltpu.VMEM)
SMEM = pl.BlockSpec(memory_space=pltpu.SMEM)
HBM = pl.BlockSpec(memory_space=pltpu.HBM)
PARAMS = pltpu.CompilerParams(vmem_limit_bytes=16 << 20)


def arrange(kernel, place, own, other, steps, shape, name, *after):
    return pl.pallas_call(
        functools.partial(kernel, per_core=steps // 2),
        out_shape=tuple([jax.ShapeDtypeStruct(shape, jnp.bfloat16)] * steps),
        in_specs=[SMEM] + [HBM] * (2 + len(after)),
        out_specs=tuple([HBM] * steps),
        scratch_shapes=[pltpu.SemaphoreType.DMA((steps,))],
        compiler_params=PARAMS,
        cost_estimate=pl.CostEstimate(
            flops=0, transcendentals=0, bytes_accessed=4 * steps * shape[0] * shape[1]
        ),
        name=name,
    )(place, own, other, *after)


def couple(cols, pieces, source, c, step, slots):
    lines, tall, block = c.shape
    return pl.pallas_call(
        functools.partial(couple_kernel, step=step, slots=slots),
        out_shape=jax.ShapeDtypeStruct((pieces.shape[1], lines * tall // slots), jnp.bfloat16),
        in_specs=[SMEM, VMEM, VMEM, VMEM],
        out_specs=VMEM,
        compiler_params=PARAMS,
        name="couple",
    )(cols, pieces, source, c)


def apply_factor(place, pieces, factor, peers):
    first = not isinstance(pieces, list)
    probes = pieces.shape[1] if first else pieces[0].shape[0]
    rows = factor.shape[0]
    shapes = [jax.ShapeDtypeStruct((probes, rows), jnp.bfloat16)]
    if peers:
        shapes.append(jax.ShapeDtypeStruct((peers, probes, rows), jnp.bfloat16))
    kernel = first_kernel if first else functools.partial(apply_kernel, lines=len(pieces))
    operands = (pieces, factor) if first else (place, *pieces, factor)
    return pl.pallas_call(
        kernel,
        out_shape=tuple(shapes),
        in_specs=[VMEM, VMEM] if first else [SMEM] + [VMEM] * (len(pieces) + 1),
        out_specs=tuple([VMEM] * len(shapes)),
        compiler_params=PARAMS,
        name="apply",
    )(*operands)


def line(value, axis):
    size = lax.axis_size(axis)
    moved = {
        k: lax.ppermute(value, axis, [(i, (i + k) % size) for i in range(size)])
        for k in range(1, size)
    }
    return [value] + [moved[k] for k in range(1, size)]


def swap(value):
    return lax.ppermute(value, "core", [(0, 1), (1, 0)])


def shards(
    signs, border_signs, inverse_factors, couplings, coupling_cols, border_rows, border_inverse
):
    local_probes, own_steps, local = signs.shape
    cores, turns = lax.axis_size("core"), lax.axis_size("zl")
    peers = lax.axis_size("zh") * lax.axis_size("y")
    probes = local_probes // cores
    steps = own_steps * cores
    core = lax.axis_index("core")
    first = core == 0
    place = jnp.stack([core, lax.axis_index("zh"), lax.axis_index("y")]).astype(jnp.int32)

    def in_order(own, other):
        return jnp.concatenate([jnp.where(first, own, other), jnp.where(first, other, own)], axis=0)

    source = (2 * signs - 1).astype(jnp.bfloat16).reshape(cores, probes, own_steps, local)
    source = source.transpose(0, 2, 1, 3)
    other_half = swap(jnp.where(first, source[1], source[0]))
    source = in_order(jnp.where(first, source[0], source[1]), other_half)
    spread = jnp.broadcast_to(source[0][None], (peers, probes, local))
    begin = lax.all_to_all(spread, NODES, 0, 0)
    slots, block = couplings.shape[2:4]
    cols = in_order(coupling_cols, swap(coupling_cols)).reshape(1, -1).astype(jnp.bfloat16)
    width = cols.shape[1]
    cols = jnp.pad(cols, ((0, 15), (0, block - width)))
    flat = source.reshape(steps * probes, local)
    halves = [flat[:, i : i + block] for i in range(0, local, block)]
    bundle = jnp.concatenate([couplings.reshape(-1, block)] + halves + [cols], axis=0)
    shared = lax.all_gather(bundle, "zh", axis=0)
    at = couplings.size // block
    until = at + steps * probes * local // block
    tall = at // own_steps

    factors = arrange(
        factor_kernel, place, inverse_factors, swap(inverse_factors), steps, inverse_factors.shape[1:], "factors"
    )

    pieces = None
    for turn in range(turns):
        results = []
        for step in range(steps):
            if pieces is None:
                resid = begin
            else:
                resid = line(couple(cols, pieces, source, blocks[step], step, slots), "y")
            more = step + 1 < steps
            outs = apply_factor(place, resid, factors[step], peers if more else 0)
            results.append(outs[0])
            if turn + step == 0:
                shared, after = lax.optimization_barrier((shared, outs[0]))
                source = shared[:, at:until]
                cols = shared[:, until, :width].astype(jnp.int32)
                blocks = arrange(
                    coupling_kernel, place, shared, swap(shared), steps, (shared.shape[0], tall, block), "couplings", after
                )
            if more:
                pieces = lax.all_to_all(outs[1], NODES, 0, 0)
        if turn + 1 < turns:
            moved = lax.ppermute(outs[0], "zl", [(turn, turn + 1)])
            pieces = lax.all_to_all(jnp.broadcast_to(moved[None], (peers, probes, local)), NODES, 0, 0)

    rows4 = in_order(border_rows, swap(border_rows))
    partial = jnp.zeros((probes, border_rows.shape[1]), jnp.float32)
    for step in range(steps):
        partial = partial + lax.dot_general(results[step], rows4[step], NT, preferred_element_type=jnp.float32)
    for axis in ("y", "zh", "zl"):
        partial = functools.reduce(jnp.add, line(partial, axis))
    halves = border_signs.reshape(cores, probes, -1)
    border_source = (2 * jnp.where(first, halves[0], halves[1]) - 1).astype(jnp.float32)
    border_resid = (border_source - partial).astype(jnp.bfloat16)
    own_border = lax.dot_general(border_resid, border_inverse, NT, preferred_element_type=jnp.float32)
    border_solved = in_order(own_border, swap(own_border))

    solved4 = jnp.stack(results)
    mine = jnp.where(first, solved4[:own_steps], solved4[own_steps:])
    theirs = swap(jnp.where(first, solved4[own_steps:], solved4[:own_steps]))
    solved = jnp.concatenate([jnp.where(first, mine, theirs), jnp.where(first, theirs, mine)], axis=1)
    solved = solved.transpose(1, 0, 2)

    total_probes = local_probes * lax.axis_size("x")
    node_sums = jnp.sum(jnp.square(solved.astype(jnp.float32)), axis=0)
    border_sums = jnp.sum(jnp.square(border_solved), axis=0)
    node_sums, border_sums = lax.psum((node_sums, border_sums), "x")
    return solved, border_solved, node_sums / total_probes, border_sums / total_probes


def solution(mesh):
    sizes = mesh.shape
    devices = mesh.devices.reshape(2, sizes["chain"] // 2, 4, sizes["mesh"] // 4, sizes["probe"])
    return jax.shard_map(
        shards,
        mesh=Mesh(devices, AXES),
        in_specs=(
            P("x", CHAIN, NODES),
            P("x", None),
            P(CHAIN, NODES, None),
            P(CHAIN, NODES, None, None, None),
            P(CHAIN, NODES, None),
            P(CHAIN, None, NODES),
            P(),
        ),
        out_specs=(P("x", CHAIN, NODES), P("x", None), P(CHAIN, NODES), P()),
        check_vma=False,
    )
```

```python
import functools

import jax
import jax.numpy as jnp
from jax import lax
from jax.experimental import pallas as pl
from jax.experimental.pallas import tpu as pltpu
from jax.sharding import Mesh, PartitionSpec as P

AXES = ("zl", "core", "zh", "y", "x")
CHAIN, NODES = ("zl", "core"), ("zh", "y")
NT = (((1,), (1,)), ((), ()))


def start_one_of(use_first, first, second):
    @pl.when(use_first)
    def _():
        for copy in first:
            copy.start()

    @pl.when(jnp.logical_not(use_first))
    def _():
        for copy in second:
            copy.start()


def arrange_kernel(place, *refs, per_core, steps, pieces, slices):
    own_refs, other_refs = refs[:pieces], refs[pieces : 2 * pieces]
    outs, sems = refs[-1 - steps : -1], refs[-1]

    def copies(refs, step):
        return [
            pltpu.make_async_copy(*slices(ref, k, outs[step], step % per_core), sems.at[step, k])
            for k, ref in enumerate(refs)
        ]

    waits = []
    for step in range(steps):
        own, other = copies(own_refs, step), copies(other_refs, step)
        start_one_of(place[0] == step // per_core, own, other)
        waits += own
    for copy in waits:
        copy.wait()


def factor_slices(ref, k, out, i):
    return ref.at[i], out


def coupling_slices(ref, k, out, i):
    size = out.shape[1]
    return ref.at[pl.ds(i * size, size)], out.at[k]


def couple_kernel(place, cols, x_ref, s_ref, c_ref, out_ref, *, step, slots):
    lines, tall, block = c_ref.shape
    rows = tall // (slots * block)
    per = x_ref.shape[2] // block
    probes = x_ref.shape[1]

    def body(k, carry):
        for row in range(rows):
            total = None
            for slot in range(0, slots, 2):
                left, right = [], []
                for pair in range(2):
                    col = cols[k, (step * rows + row) * slots + slot + pair]
                    lanes = pl.ds(pl.multiple_of((col % per) * block, block), block)
                    left.append(x_ref[col // per, :, lanes])
                    at = (row * slots + slot + pair) * block
                    right.append(c_ref[k, at : at + block, :])
                term = lax.dot_general(
                    jnp.concatenate(left, axis=1),
                    jnp.concatenate(right, axis=1),
                    NT,
                    preferred_element_type=jnp.float32,
                )
                total = term if total is None else total + term
            at = (row * s_ref.shape[1]) // rows + step * probes
            source = s_ref[k, at : at + probes, :].astype(jnp.float32)
            home = lax.rem(place[1] + lines - k, lines)
            lanes = pl.ds(pl.multiple_of((home * rows + row) * block, block), block)
            out_ref[:, lanes] = (source - total).astype(jnp.bfloat16)
        return carry

    lax.fori_loop(0, lines, body, 0)


def finish(total, outs):
    result = total.astype(jnp.bfloat16)
    outs[0][...] = result
    if len(outs) > 1:
        for peer in range(outs[1].shape[0]):
            outs[1][peer] = result


def early_kernel(place, r_ref, own_ref, other_ref, *refs, step, per_core):
    outs, (l_buf, sems) = refs[:-2], refs[-2:]
    chunks, _, wide = l_buf.shape
    own, other = (
        [
            pltpu.make_async_copy(
                source.at[step % per_core, :, pl.ds(i * wide, wide)], l_buf.at[i], sems.at[i]
            )
            for i in range(chunks)
        ]
        for source in (own_ref, other_ref)
    )
    start_one_of(place[0] == step // per_core, own, other)
    width = r_ref.shape[2]
    per = wide // width
    total = jnp.zeros((r_ref.shape[1], l_buf.shape[1]), jnp.float32)
    for i in range(chunks):
        own[i].wait()
        left = jnp.concatenate([r_ref[i * per + j] for j in range(per)], axis=1)
        total = total + lax.dot_general(left, l_buf[i], NT, preferred_element_type=jnp.float32)
    finish(total, outs)


def early_couple_kernel(place, cols, x_ref, s_ref, own_ref, other_ref, out_ref, c_buf, sem, *, step, per_core):
    rows, slots, block, _ = c_buf.shape
    own, other = (
        [pltpu.make_async_copy(source.at[step % per_core], c_buf, sem)] for source in (own_ref, other_ref)
    )
    start_one_of(place[0] == step // per_core, own, other)
    own[0].wait()
    per = x_ref.shape[2] // block
    for row in range(rows):
        total = None
        for slot in range(slots):
            col = cols[(step * rows + row) * slots + slot]
            lanes = pl.ds(pl.multiple_of((col % per) * block, block), block)
            term = lax.dot_general(
                x_ref[col // per, :, lanes], c_buf[row, slot], NT, preferred_element_type=jnp.float32
            )
            total = term if total is None else total + term
        span = slice(row * block, (row + 1) * block)
        resid = (s_ref[:, span].astype(jnp.float32) - total).astype(jnp.bfloat16)
        for peer in range(out_ref.shape[0]):
            out_ref[peer, :, span] = resid


def apply_kernel(place, *refs, lines):
    pieces, l_ref, outs = refs[:lines], refs[lines], refs[lines + 1 :]
    width = l_ref.shape[0]

    def body(zh, total):
        for k in range(lines):
            y = lax.rem(place[2] + lines - k, lines)
            lanes = pl.ds(pl.multiple_of((zh * lines + y) * width, width), width)
            here = pl.ds(pl.multiple_of(zh * width, width), width)
            total = total + lax.dot_general(
                pieces[k][:, here], l_ref[:, lanes], NT, preferred_element_type=jnp.float32
            )
        return total

    start = jnp.zeros((pieces[0].shape[0], width), jnp.float32)
    finish(lax.fori_loop(0, pieces[0].shape[1] // width, body, start), outs)


VMEM = pl.BlockSpec(memory_space=pltpu.VMEM)
SMEM = pl.BlockSpec(memory_space=pltpu.SMEM)
HBM = pl.BlockSpec(memory_space=pltpu.HBM)
PARAMS = pltpu.CompilerParams(vmem_limit_bytes=16 << 20)


def arrange(slices, place, own, other, steps, shape, name, after):
    pieces = len(own)
    return pl.pallas_call(
        functools.partial(
            arrange_kernel, per_core=steps // 2, steps=steps, pieces=pieces, slices=slices
        ),
        out_shape=tuple([jax.ShapeDtypeStruct(shape, jnp.bfloat16)] * steps),
        in_specs=[SMEM] + [HBM] * (2 * pieces + 1),
        out_specs=tuple([HBM] * steps),
        scratch_shapes=[pltpu.SemaphoreType.DMA((steps, pieces))],
        compiler_params=PARAMS,
        cost_estimate=pl.CostEstimate(
            flops=0, transcendentals=0, bytes_accessed=4 * steps * shape[0] * shape[1]
        ),
        name=name,
    )(place, *own, *other, after)


def couple(place, cols, pieces, source, c, step, slots):
    lines, tall, block = c.shape
    return pl.pallas_call(
        functools.partial(couple_kernel, step=step, slots=slots),
        out_shape=jax.ShapeDtypeStruct((pieces.shape[1], lines * tall // slots), jnp.bfloat16),
        in_specs=[SMEM, SMEM, VMEM, VMEM, VMEM],
        out_specs=VMEM,
        compiler_params=PARAMS,
        name="couple",
    )(place, cols, pieces, source, c)


def solved_shapes(probes, rows, peers):
    shapes = [jax.ShapeDtypeStruct((probes, rows), jnp.bfloat16)]
    if peers:
        shapes.append(jax.ShapeDtypeStruct((peers, probes, rows), jnp.bfloat16))
    return tuple(shapes)


def apply_factor(place, pieces, factor, peers):
    shapes = solved_shapes(pieces[0].shape[0], factor.shape[0], peers)
    return pl.pallas_call(
        functools.partial(apply_kernel, lines=len(pieces)),
        out_shape=shapes,
        in_specs=[SMEM] + [VMEM] * (len(pieces) + 1),
        out_specs=tuple([VMEM] * len(shapes)),
        compiler_params=PARAMS,
        name="apply",
    )(place, *pieces, factor)


def apply_early(place, pieces, own, other, step):
    peers, probes, _ = pieces.shape
    per_core, rows, width = own.shape
    shapes = solved_shapes(probes, rows, peers)
    return pl.pallas_call(
        functools.partial(early_kernel, step=step, per_core=per_core),
        out_shape=shapes,
        in_specs=[SMEM, VMEM, HBM, HBM],
        out_specs=tuple([VMEM] * len(shapes)),
        scratch_shapes=[
            pltpu.VMEM((4, rows, width // 4), own.dtype),
            pltpu.SemaphoreType.DMA((4,)),
        ],
        compiler_params=PARAMS,
        name="apply_early",
    )(place, pieces, own, other)


def couple_early(place, cols, pieces, source, own, other, step):
    return pl.pallas_call(
        functools.partial(early_couple_kernel, step=step, per_core=own.shape[0]),
        out_shape=jax.ShapeDtypeStruct(pieces.shape, jnp.bfloat16),
        in_specs=[SMEM, SMEM, VMEM, VMEM, HBM, HBM],
        out_specs=VMEM,
        scratch_shapes=[pltpu.VMEM(own.shape[1:], own.dtype), pltpu.SemaphoreType.DMA],
        compiler_params=PARAMS,
        name="couple_early",
    )(place, cols, pieces, source, own, other)


def line(value, axis):
    size = lax.axis_size(axis)
    moved = {
        k: lax.ppermute(value, axis, [(i, (i + k) % size) for i in range(size)])
        for k in range(1, size)
    }
    return [value] + [moved[k] for k in range(1, size)]


def swap(value):
    return lax.ppermute(value, "core", [(0, 1), (1, 0)])


def shards(
    signs, border_signs, inverse_factors, couplings, coupling_cols, border_rows, border_inverse
):
    local_probes, own_steps, local = signs.shape
    cores, turns = lax.axis_size("core"), lax.axis_size("zl")
    peers = lax.axis_size("zh") * lax.axis_size("y")
    probes = local_probes // cores
    steps = own_steps * cores
    core = lax.axis_index("core")
    first = core == 0
    place = jnp.stack([core, lax.axis_index("zh"), lax.axis_index("y")]).astype(jnp.int32)

    def in_order(own, other):
        return jnp.concatenate([jnp.where(first, own, other), jnp.where(first, other, own)], axis=0)

    source = (2 * signs - 1).astype(jnp.bfloat16).reshape(cores, probes, own_steps, local)
    source = source.transpose(0, 2, 1, 3)
    other_half = swap(jnp.where(first, source[1], source[0]))
    own_source = in_order(jnp.where(first, source[0], source[1]), other_half)
    spread = jnp.broadcast_to(own_source[0][None], (peers, probes, local))
    own_cols = in_order(coupling_cols, swap(coupling_cols)).reshape(-1)
    other_factors, other_couplings = swap(inverse_factors), swap(couplings)

    def everywhere(value):
        return lax.all_to_all(value, NODES, 0, 0)

    solved0 = apply_early(place, everywhere(spread), inverse_factors, other_factors, 0)
    slots, block = couplings.shape[2:4]
    cols = own_cols.reshape(1, -1).astype(jnp.bfloat16)
    width = cols.shape[1]
    cols = jnp.pad(cols, ((0, 15), (0, block - width)))
    flat = own_source.reshape(steps * probes, local)
    halves = [flat[:, i : i + block] for i in range(0, local, block)]
    bundle = jnp.concatenate([couplings.reshape(-1, block)] + halves + [cols], axis=0)
    shared = line(bundle, "zh")
    at = couplings.size // block
    until = at + steps * probes * local // block
    tall = at // own_steps
    resid = couple_early(
        place, own_cols, everywhere(solved0[1]), own_source[1], couplings, other_couplings, 1
    )
    solved1 = apply_early(place, everywhere(resid), inverse_factors, other_factors, 1)
    pieces = everywhere(solved1[1])
    shared, after = lax.optimization_barrier((shared, solved1[0]))
    source = jnp.stack([s[at:until] for s in shared])
    cols = jnp.concatenate([s[until : until + 1, :width] for s in shared], axis=0).astype(jnp.int32)
    shape = (len(shared), tall, block)
    blocks = arrange(
        coupling_slices, place, shared, [swap(s) for s in shared], steps, shape, "couplings", after
    )
    factors = arrange(
        factor_slices, place, [inverse_factors], [other_factors], steps, inverse_factors.shape[1:], "factors", after
    )

    for turn in range(turns):
        results = []
        for step in range(2 if turn == 0 else 0, steps):
            resid = line(couple(place, cols, pieces, source, blocks[step], step, slots), "y")
            more = step + 1 < steps
            outs = apply_factor(place, resid, factors[step], peers if more else 0)
            results.append(outs[0])
            if more:
                pieces = everywhere(outs[1])
        if turn + 1 < turns:
            moved = lax.ppermute(outs[0], "zl", [(turn, turn + 1)])
            pieces = everywhere(jnp.broadcast_to(moved[None], (peers, probes, local)))

    rows4 = in_order(border_rows, swap(border_rows))
    partial = jnp.zeros((probes, border_rows.shape[1]), jnp.float32)
    for step in range(steps):
        partial = partial + lax.dot_general(results[step], rows4[step], NT, preferred_element_type=jnp.float32)
    for axis in ("y", "zh", "zl"):
        partial = functools.reduce(jnp.add, line(partial, axis))
    halves = border_signs.reshape(cores, probes, -1)
    border_source = (2 * jnp.where(first, halves[0], halves[1]) - 1).astype(jnp.float32)
    border_resid = (border_source - partial).astype(jnp.bfloat16)
    own_border = lax.dot_general(border_resid, border_inverse, NT, preferred_element_type=jnp.float32)
    border_solved = in_order(own_border, swap(own_border))

    solved4 = jnp.stack(results)
    mine = jnp.where(first, solved4[:own_steps], solved4[own_steps:])
    theirs = swap(jnp.where(first, solved4[own_steps:], solved4[:own_steps]))
    solved = jnp.concatenate([jnp.where(first, mine, theirs), jnp.where(first, theirs, mine)], axis=1)
    solved = solved.transpose(1, 0, 2)

    total_probes = local_probes * lax.axis_size("x")
    node_sums = jnp.sum(jnp.square(solved.astype(jnp.float32)), axis=0)
    border_sums = jnp.sum(jnp.square(border_solved), axis=0)
    node_sums, border_sums = lax.psum((node_sums, border_sums), "x")
    return solved, border_solved, node_sums / total_probes, border_sums / total_probes


def solution(mesh):
    sizes = mesh.shape
    devices = mesh.devices.reshape(2, sizes["chain"] // 2, 4, sizes["mesh"] // 4, sizes["probe"])
    return jax.shard_map(
        shards,
        mesh=Mesh(devices, AXES),
        in_specs=(
            P("x", CHAIN, NODES),
            P("x", None),
            P(CHAIN, NODES, None),
            P(CHAIN, NODES, None, None, None),
            P(CHAIN, NODES, None),
            P(CHAIN, None, NODES),
            P(),
        ),
        out_specs=(P("x", CHAIN, NODES), P("x", None), P(CHAIN, NODES), P()),
        check_vma=False,
    )
```

```python
import functools

import jax
import jax.numpy as jnp
from jax import lax
from jax.experimental import pallas as pl
from jax.experimental.pallas import tpu as pltpu
from jax.sharding import Mesh, PartitionSpec as P

AXES = ("zl", "core", "zh", "y", "x")
CHAIN, NODES = ("zl", "core"), ("zh", "y")
NT = (((1,), (1,)), ((), ()))


def start_one_of(use_first, first, second):
    @pl.when(use_first)
    def _():
        for copy in first:
            copy.start()

    @pl.when(jnp.logical_not(use_first))
    def _():
        for copy in second:
            copy.start()


def arrange_kernel(place, *refs, per_core, steps, pieces, slices):
    own_refs, other_refs = refs[:pieces], refs[pieces : 2 * pieces]
    outs, sems = refs[-1 - steps : -1], refs[-1]

    def copies(refs, step):
        return [
            pltpu.make_async_copy(*slices(ref, k, outs[step], step % per_core), sems.at[step, k])
            for k, ref in enumerate(refs)
        ]

    waits = []
    for step in range(steps):
        own, other = copies(own_refs, step), copies(other_refs, step)
        start_one_of(place[0] == step // per_core, own, other)
        waits += own
    for copy in waits:
        copy.wait()


def factor_slices(ref, k, out, i):
    return ref.at[i], out


def couple_kernel(place, cols, x_ref, own_ref, other_ref, out_ref):
    lines, tall, block = other_ref.shape
    slots = tall // block
    per = x_ref.shape[2] // block
    probes = x_ref.shape[1]

    def body(k, carry):
        home = lax.rem(place[1] + lines - k, lines)
        for c_ref, row in ((own_ref, place[0]), (other_ref, 1 - place[0])):
            total = None
            for slot in range(0, slots, 2):
                left, right = [], []
                for pair in range(2):
                    col = cols[k, row * slots + slot + pair]
                    lanes = pl.ds(pl.multiple_of((col % per) * block, block), block)
                    left.append(x_ref[col // per, :, lanes])
                    at = (slot + pair) * block
                    right.append(c_ref[k, at : at + block, :])
                term = lax.dot_general(
                    jnp.concatenate(left, axis=1),
                    jnp.concatenate(right, axis=1),
                    NT,
                    preferred_element_type=jnp.float32,
                )
                total = term if total is None else total + term
            at = pl.multiple_of(tall + row * probes, probes)
            source = own_ref[k, pl.ds(at, probes), :].astype(jnp.float32)
            lanes = pl.ds(pl.multiple_of((home * per + row) * block, block), block)
            resid = (source - total).astype(jnp.bfloat16)
            for peer in range(out_ref.shape[0]):
                out_ref[peer, :, lanes] = resid
        return carry

    lax.fori_loop(0, lines, body, 0)


def finish(total, outs):
    result = total.astype(jnp.bfloat16)
    outs[0][...] = result
    if len(outs) > 1:
        for peer in range(outs[1].shape[0]):
            outs[1][peer] = result


def early_kernel(place, r_ref, own_ref, other_ref, *refs, step, per_core):
    outs, (l_buf, sems) = refs[:-2], refs[-2:]
    chunks, _, wide = l_buf.shape
    own, other = (
        [
            pltpu.make_async_copy(
                source.at[step % per_core, :, pl.ds(i * wide, wide)], l_buf.at[i], sems.at[i]
            )
            for i in range(chunks)
        ]
        for source in (own_ref, other_ref)
    )
    start_one_of(place[0] == step // per_core, own, other)
    width = r_ref.shape[2]
    per = wide // width
    total = jnp.zeros((r_ref.shape[1], l_buf.shape[1]), jnp.float32)
    for i in range(chunks):
        own[i].wait()
        left = jnp.concatenate([r_ref[i * per + j] for j in range(per)], axis=1)
        total = total + lax.dot_general(left, l_buf[i], NT, preferred_element_type=jnp.float32)
    finish(total, outs)


def apply_kernel(r_ref, l_ref, *outs):
    width = l_ref.shape[0]
    lines = r_ref.shape[0]

    def body(zh, total):
        for y in range(lines):
            lanes = pl.ds(pl.multiple_of((zh * lines + y) * width, width), width)
            here = pl.ds(pl.multiple_of(zh * width, width), width)
            total = total + lax.dot_general(
                r_ref[y, :, here], l_ref[:, lanes], NT, preferred_element_type=jnp.float32
            )
        return total

    start = jnp.zeros((r_ref.shape[1], width), jnp.float32)
    finish(lax.fori_loop(0, r_ref.shape[2] // width, body, start), outs)


VMEM = pl.BlockSpec(memory_space=pltpu.VMEM)
SMEM = pl.BlockSpec(memory_space=pltpu.SMEM)
HBM = pl.BlockSpec(memory_space=pltpu.HBM)
PARAMS = pltpu.CompilerParams(vmem_limit_bytes=16 << 20)


def arrange(slices, place, own, other, steps, shape, name, after):
    pieces = len(own)
    return pl.pallas_call(
        functools.partial(
            arrange_kernel, per_core=steps // 2, steps=steps, pieces=pieces, slices=slices
        ),
        out_shape=tuple([jax.ShapeDtypeStruct(shape, jnp.bfloat16)] * steps),
        in_specs=[SMEM] + [HBM] * (2 * pieces + 1),
        out_specs=tuple([HBM] * steps),
        scratch_shapes=[pltpu.SemaphoreType.DMA((steps, pieces))],
        compiler_params=PARAMS,
        cost_estimate=pl.CostEstimate(
            flops=0, transcendentals=0, bytes_accessed=4 * steps * shape[0] * shape[1]
        ),
        name=name,
    )(place, *own, *other, after)


def couple(place, pieces, shared, receivers):
    cols, own, other = shared
    lines, tall, block = other.shape
    per = pieces.shape[2] // block
    return pl.pallas_call(
        couple_kernel,
        out_shape=jax.ShapeDtypeStruct((receivers, pieces.shape[1], lines * per * block), jnp.bfloat16),
        in_specs=[SMEM, SMEM, VMEM, VMEM, VMEM],
        out_specs=VMEM,
        compiler_params=PARAMS,
        name="couple",
    )(place, cols, pieces, own, other)


def solved_shapes(probes, rows, peers):
    shapes = [jax.ShapeDtypeStruct((probes, rows), jnp.bfloat16)]
    if peers:
        shapes.append(jax.ShapeDtypeStruct((peers, probes, rows), jnp.bfloat16))
    return tuple(shapes)


def apply_factor(pieces, factor, peers):
    shapes = solved_shapes(pieces.shape[1], factor.shape[0], peers)
    return pl.pallas_call(
        apply_kernel,
        out_shape=shapes,
        in_specs=[VMEM, VMEM],
        out_specs=tuple([VMEM] * len(shapes)),
        compiler_params=PARAMS,
        name="apply",
    )(pieces, factor)


def apply_early(place, pieces, own, other, step):
    peers, probes, _ = pieces.shape
    per_core, rows, width = own.shape
    shapes = solved_shapes(probes, rows, peers)
    return pl.pallas_call(
        functools.partial(early_kernel, step=step, per_core=per_core),
        out_shape=shapes,
        in_specs=[SMEM, VMEM, HBM, HBM],
        out_specs=tuple([VMEM] * len(shapes)),
        scratch_shapes=[
            pltpu.VMEM((4, rows, width // 4), own.dtype),
            pltpu.SemaphoreType.DMA((4,)),
        ],
        compiler_params=PARAMS,
        name="apply_early",
    )(place, pieces, own, other)


def line(value, axis):
    size = lax.axis_size(axis)
    moved = {
        k: lax.ppermute(value, axis, [(i, (i + k) % size) for i in range(size)])
        for k in range(1, size)
    }
    return [value] + [moved[k] for k in range(1, size)]


def swap(value):
    return lax.ppermute(value, "core", [(0, 1), (1, 0)])


def shards(
    signs, border_signs, inverse_factors, couplings, coupling_cols, border_rows, border_inverse
):
    local_probes, own_steps, local = signs.shape
    cores, turns = lax.axis_size("core"), lax.axis_size("zl")
    peers = lax.axis_size("zh") * lax.axis_size("y")
    probes = local_probes // cores
    steps = own_steps * cores
    core = lax.axis_index("core")
    first = core == 0
    place = jnp.stack([core, lax.axis_index("zh"), lax.axis_index("y")]).astype(jnp.int32)

    def in_order(own, other):
        return jnp.concatenate([jnp.where(first, own, other), jnp.where(first, other, own)], axis=0)

    source = (2 * signs - 1).astype(jnp.bfloat16).reshape(cores, probes, own_steps, local)
    source = source.transpose(0, 2, 1, 3)
    own_cols = jnp.pad(coupling_cols.reshape(own_steps, 1, -1), ((0, 0), (0, 15), (0, local - coupling_cols[0].size)))

    def packed(half):
        return jnp.concatenate([half, own_cols.astype(jnp.bfloat16)], axis=1)

    other_half = swap(packed(jnp.where(first, source[1], source[0])))
    both = in_order(packed(jnp.where(first, source[0], source[1])), other_half)
    own_source = both[:, :probes]
    spread = jnp.broadcast_to(own_source[0][None], (peers, probes, local))
    other_factors, other_couplings = swap(inverse_factors), swap(couplings)
    slots, block = couplings.shape[2:4]
    tall, width = slots * block, 2 * slots

    def everywhere(value):
        return lax.all_to_all(value, NODES, 0, 0)

    def send(step, after):
        i = step % own_steps
        own_c, other_c, _ = lax.optimization_barrier((couplings[i], other_couplings[i], after))
        low = first if step < own_steps else jnp.logical_not(first)
        rows = jnp.where(low, own_c, other_c).reshape(2, tall, block)
        mine, theirs = jnp.where(first, rows[0], rows[1]), jnp.where(first, rows[1], rows[0])
        tail = both[step, probes:, :block]
        halves = [own_source[step, :, j : j + block] for j in range(0, local, block)]
        return line(jnp.concatenate([mine] + halves + [tail], axis=0), "zh"), theirs

    def receive(sent, after):
        bundles, theirs = sent
        bundles, theirs, _ = lax.optimization_barrier((bundles, theirs, after))
        own = jnp.stack(bundles)
        other = jnp.concatenate([theirs[None], swap(own[1:, :tall])], axis=0)
        cols = own[:, -16, :width].astype(jnp.int32)
        return cols, own, other

    sent, shared = {}, {}
    sent[1] = send(1, spread)
    outs = apply_early(place, everywhere(spread), inverse_factors, other_factors, 0)
    factors = arrange(
        factor_slices, place, [inverse_factors], [other_factors], steps, inverse_factors.shape[1:], "factors", outs[0]
    )
    shared[1] = receive(sent[1], outs[0])
    sent[2] = send(2, outs[0])
    pieces = everywhere(outs[1])
    for turn in range(turns):
        results = []
        for step in range(1 if turn == 0 else 0, steps):
            resid = lax.all_to_all(couple(place, pieces, shared[step], lax.axis_size("y")), "y", 0, 0)
            more = step + 1 < steps
            outs = apply_factor(resid, factors[step], peers if more else 0)
            results.append(outs[0])
            if turn == 0:
                later, following = (step + 1) % steps, (step + 2) % steps
                shared[later] = receive(sent[later], outs[0])
                if following != 1:
                    sent[following] = send(following, outs[0])
            if more:
                pieces = everywhere(outs[1])
        if turn + 1 < turns:
            moved = lax.ppermute(outs[0], "zl", [(turn, turn + 1)])
            pieces = everywhere(jnp.broadcast_to(moved[None], (peers, probes, local)))

    rows4 = in_order(border_rows, swap(border_rows))
    partial = jnp.zeros((probes, border_rows.shape[1]), jnp.float32)
    for step in range(steps):
        partial = partial + lax.dot_general(results[step], rows4[step], NT, preferred_element_type=jnp.float32)
    for axis in ("y", "zh", "zl"):
        partial = functools.reduce(jnp.add, line(partial, axis))
    halves = border_signs.reshape(cores, probes, -1)
    border_source = (2 * jnp.where(first, halves[0], halves[1]) - 1).astype(jnp.float32)
    border_resid = (border_source - partial).astype(jnp.bfloat16)
    own_border = lax.dot_general(border_resid, border_inverse, NT, preferred_element_type=jnp.float32)
    border_solved = in_order(own_border, swap(own_border))

    solved4 = jnp.stack(results)
    mine = jnp.where(first, solved4[:own_steps], solved4[own_steps:])
    theirs = swap(jnp.where(first, solved4[own_steps:], solved4[:own_steps]))
    solved = jnp.concatenate([jnp.where(first, mine, theirs), jnp.where(first, theirs, mine)], axis=1)
    solved = solved.transpose(1, 0, 2)

    total_probes = local_probes * lax.axis_size("x")
    node_sums = jnp.sum(jnp.square(solved.astype(jnp.float32)), axis=0)
    border_sums = jnp.sum(jnp.square(border_solved), axis=0)
    node_sums, border_sums = lax.psum((node_sums, border_sums), "x")
    return solved, border_solved, node_sums / total_probes, border_sums / total_probes


def solution(mesh):
    sizes = mesh.shape
    devices = mesh.devices.reshape(2, sizes["chain"] // 2, 4, sizes["mesh"] // 4, sizes["probe"])
    return jax.shard_map(
        shards,
        mesh=Mesh(devices, AXES),
        in_specs=(
            P("x", CHAIN, NODES),
            P("x", None),
            P(CHAIN, NODES, None),
            P(CHAIN, NODES, None, None, None),
            P(CHAIN, NODES, None),
            P(CHAIN, None, NODES),
            P(),
        ),
        out_specs=(P("x", CHAIN, NODES), P("x", None), P(CHAIN, NODES), P()),
        check_vma=False,
    )
```

```python
import functools

import jax
import jax.numpy as jnp
from jax import lax
from jax.experimental import pallas as pl
from jax.experimental.pallas import tpu as pltpu
from jax.sharding import Mesh, PartitionSpec as P

AXES = ("zl", "core", "zh", "y", "x")
CHAIN, NODES = ("zl", "core"), ("zh", "y")
NT = (((1,), (1,)), ((), ()))


def start_one_of(use_first, first, second):
    @pl.when(use_first)
    def _():
        for copy in first:
            copy.start()

    @pl.when(jnp.logical_not(use_first))
    def _():
        for copy in second:
            copy.start()


def full_kernel(
    place, cols, x_ref, own_c, other_c, own_l, other_l, *refs, step, per_core, slots
):
    outs, (c_buf, s_buf, r_buf, l_buf, c_sems, s_sems, l_sems) = refs[:-7], refs[-7:]
    peers, tall, block = c_buf.shape
    probes, width = x_ref.shape[1:]
    per = width // block
    chunks, _, wide = l_buf.shape
    i = step % per_core
    own, other = (
        [pltpu.make_async_copy(c.at[m, pl.ds(i * tall, tall)], c_buf.at[m], c_sems.at[m]) for m in range(peers)]
        + [pltpu.make_async_copy(f.at[i, :, pl.ds(j * wide, wide)], l_buf.at[j], l_sems.at[j]) for j in range(chunks)]
        for c, f in ((own_c, own_l), (other_c, other_l))
    )
    begin, steps = per_core * tall, 2 * per_core
    sources = [
        pltpu.make_async_copy(
            own_c.at[:, pl.ds(begin + (half * steps + step) * probes, probes)], s_buf.at[half], s_sems.at[half]
        )
        for half in range(per)
    ]
    for copy in sources:
        copy.start()
    start_one_of(place[0] == step // per_core, own, other)
    for copy in sources:
        copy.wait()
    for m in range(peers):
        own[m].wait()

    def body(m, carry):
        for row in range(per):
            total = None
            for slot in range(0, slots, 2):
                left, right = [], []
                for pair in range(2):
                    col = cols[m, (step * per + row) * slots + slot + pair]
                    lanes = pl.ds(pl.multiple_of((col % per) * block, block), block)
                    left.append(x_ref[col // per, :, lanes])
                    at = (row * slots + slot + pair) * block
                    right.append(c_buf[m, at : at + block, :])
                term = lax.dot_general(
                    jnp.concatenate(left, axis=1),
                    jnp.concatenate(right, axis=1),
                    NT,
                    preferred_element_type=jnp.float32,
                )
                total = term if total is None else total + term
            resid = s_buf[row, m].astype(jnp.float32) - total
            r_buf[m, :, row * block : (row + 1) * block] = resid.astype(jnp.bfloat16)
        return carry

    lax.fori_loop(0, peers, body, 0, unroll=2)
    group = peers // chunks
    total = jnp.zeros((probes, l_buf.shape[1]), jnp.float32)
    for j in range(chunks):
        own[peers + j].wait()
        left = jnp.concatenate([r_buf[j * group + n] for n in range(group)], axis=1)
        total = total + lax.dot_general(left, l_buf[j], NT, preferred_element_type=jnp.float32)
    finish(total, outs)


def finish(total, outs):
    result = total.astype(jnp.bfloat16)
    outs[0][...] = result
    if len(outs) > 1:
        for peer in range(outs[1].shape[0]):
            outs[1][peer] = result


def early_kernel(place, r_ref, own_ref, other_ref, *refs, step, per_core):
    outs, (l_buf, sems) = refs[:-2], refs[-2:]
    chunks, _, wide = l_buf.shape
    own, other = (
        [
            pltpu.make_async_copy(
                source.at[step % per_core, :, pl.ds(i * wide, wide)], l_buf.at[i], sems.at[i]
            )
            for i in range(chunks)
        ]
        for source in (own_ref, other_ref)
    )
    start_one_of(place[0] == step // per_core, own, other)
    width = r_ref.shape[2]
    per = wide // width
    total = jnp.zeros((r_ref.shape[1], l_buf.shape[1]), jnp.float32)
    for i in range(chunks):
        own[i].wait()
        left = jnp.concatenate([r_ref[i * per + j] for j in range(per)], axis=1)
        total = total + lax.dot_general(left, l_buf[i], NT, preferred_element_type=jnp.float32)
    finish(total, outs)


def early_couple_kernel(place, cols, x_ref, s_ref, own_ref, other_ref, out_ref, c_buf, sem, *, step, per_core):
    rows, slots, block, _ = c_buf.shape
    own, other = (
        [pltpu.make_async_copy(source.at[step % per_core], c_buf, sem)] for source in (own_ref, other_ref)
    )
    start_one_of(place[0] == step // per_core, own, other)
    own[0].wait()
    per = x_ref.shape[2] // block
    for row in range(rows):
        total = None
        for slot in range(slots):
            col = cols[(step * rows + row) * slots + slot]
            lanes = pl.ds(pl.multiple_of((col % per) * block, block), block)
            term = lax.dot_general(
                x_ref[col // per, :, lanes], c_buf[row, slot], NT, preferred_element_type=jnp.float32
            )
            total = term if total is None else total + term
        span = slice(row * block, (row + 1) * block)
        resid = (s_ref[:, span].astype(jnp.float32) - total).astype(jnp.bfloat16)
        for peer in range(out_ref.shape[0]):
            out_ref[peer, :, span] = resid


VMEM = pl.BlockSpec(memory_space=pltpu.VMEM)
SMEM = pl.BlockSpec(memory_space=pltpu.SMEM)
HBM = pl.BlockSpec(memory_space=pltpu.HBM)
PARAMS = pltpu.CompilerParams(vmem_limit_bytes=50 << 20)


def solved_shapes(probes, rows, peers):
    shapes = [jax.ShapeDtypeStruct((probes, rows), jnp.bfloat16)]
    if peers:
        shapes.append(jax.ShapeDtypeStruct((peers, probes, rows), jnp.bfloat16))
    return tuple(shapes)


def apply_full(place, cols, pieces, shared, factors, step, slots, block, spread):
    peers, probes, width = pieces.shape
    per_core, rows, whole = factors[0].shape
    per = width // block
    shapes = solved_shapes(probes, rows, peers if spread else 0)
    return pl.pallas_call(
        functools.partial(full_kernel, step=step, per_core=per_core, slots=slots),
        out_shape=shapes,
        in_specs=[SMEM, SMEM, VMEM] + [HBM] * 4,
        out_specs=tuple([VMEM] * len(shapes)),
        scratch_shapes=[
            pltpu.VMEM((peers, per * slots * block, block), jnp.bfloat16),
            pltpu.VMEM((per, peers, probes, block), jnp.bfloat16),
            pltpu.VMEM((peers, probes, width), jnp.bfloat16),
            pltpu.VMEM((4, rows, whole // 4), jnp.bfloat16),
            pltpu.SemaphoreType.DMA((peers,)),
            pltpu.SemaphoreType.DMA((per,)),
            pltpu.SemaphoreType.DMA((4,)),
        ],
        compiler_params=PARAMS,
        name="apply_full",
    )(place, cols, pieces, *shared, *factors)


def apply_early(place, pieces, own, other, step):
    peers, probes, _ = pieces.shape
    per_core, rows, width = own.shape
    shapes = solved_shapes(probes, rows, peers)
    return pl.pallas_call(
        functools.partial(early_kernel, step=step, per_core=per_core),
        out_shape=shapes,
        in_specs=[SMEM, VMEM, HBM, HBM],
        out_specs=tuple([VMEM] * len(shapes)),
        scratch_shapes=[
            pltpu.VMEM((4, rows, width // 4), own.dtype),
            pltpu.SemaphoreType.DMA((4,)),
        ],
        compiler_params=PARAMS,
        name="apply_early",
    )(place, pieces, own, other)


def couple_early(place, cols, pieces, source, own, other, step):
    return pl.pallas_call(
        functools.partial(early_couple_kernel, step=step, per_core=own.shape[0]),
        out_shape=jax.ShapeDtypeStruct(pieces.shape, jnp.bfloat16),
        in_specs=[SMEM, SMEM, VMEM, VMEM, HBM, HBM],
        out_specs=VMEM,
        scratch_shapes=[pltpu.VMEM(own.shape[1:], own.dtype), pltpu.SemaphoreType.DMA],
        compiler_params=PARAMS,
        name="couple_early",
    )(place, cols, pieces, source, own, other)


def line(value, axis):
    size = lax.axis_size(axis)
    moved = {
        k: lax.ppermute(value, axis, [(i, (i + k) % size) for i in range(size)])
        for k in range(1, size)
    }
    return [value] + [moved[k] for k in range(1, size)]


def swap(value):
    return lax.ppermute(value, "core", [(0, 1), (1, 0)])


def shards(
    signs, border_signs, inverse_factors, couplings, coupling_cols, border_rows, border_inverse
):
    local_probes, own_steps, local = signs.shape
    cores, turns = lax.axis_size("core"), lax.axis_size("zl")
    peers = lax.axis_size("zh") * lax.axis_size("y")
    probes = local_probes // cores
    steps = own_steps * cores
    core = lax.axis_index("core")
    first = core == 0
    place = jnp.stack([core, lax.axis_index("zh"), lax.axis_index("y")]).astype(jnp.int32)

    def in_order(own, other):
        return jnp.concatenate([jnp.where(first, own, other), jnp.where(first, other, own)], axis=0)

    source = (2 * signs - 1).astype(jnp.bfloat16).reshape(cores, probes, own_steps, local)
    source = source.transpose(0, 2, 1, 3)
    other_half = swap(jnp.where(first, source[1], source[0]))
    own_source = in_order(jnp.where(first, source[0], source[1]), other_half)
    spread = jnp.broadcast_to(own_source[0][None], (peers, probes, local))
    own_cols = in_order(coupling_cols, swap(coupling_cols)).reshape(-1)
    other_factors, other_couplings = swap(inverse_factors), swap(couplings)

    def everywhere(value):
        return lax.all_to_all(value, NODES, 0, 0)

    slots, block = couplings.shape[2:4]
    cols = own_cols.reshape(1, -1).astype(jnp.bfloat16)
    width = cols.shape[1]
    cols = jnp.pad(cols, ((0, 15), (0, block - width)))
    flat = own_source.reshape(steps * probes, local)
    halves = [flat[:, i : i + block] for i in range(0, local, block)]
    bundle = jnp.concatenate([couplings.reshape(-1, block)] + halves + [cols], axis=0)
    shared = lax.all_gather(bundle, NODES, axis=0)
    factors = (inverse_factors, other_factors)

    results = []
    resid = spread
    for step in range(steps):
        outs = apply_early(place, everywhere(resid), *factors, step)
        if step + 1 < steps:
            pieces = everywhere(outs[1])
            resid = couple_early(
                place, own_cols, pieces, own_source[step + 1], couplings, other_couplings, step + 1
            )
        if step == 2:
            shared, _, resid = lax.optimization_barrier((shared, outs[0], resid))
            full = (shared, swap(shared))
    until = couplings.size // block + steps * probes * local // block
    cols = shared[:, until, :width].astype(jnp.int32)
    for turn in range(1, turns):
        moved = lax.ppermute(outs[0], "zl", [(turn - 1, turn)])
        pieces = everywhere(jnp.broadcast_to(moved[None], (peers, probes, local)))
        results = []
        for step in range(steps):
            more = step + 1 < steps
            outs = apply_full(place, cols, pieces, full, factors, step, slots, block, more)
            results.append(outs[0])
            if more:
                pieces = everywhere(outs[1])

    rows4 = in_order(border_rows, swap(border_rows))
    partial = jnp.zeros((probes, border_rows.shape[1]), jnp.float32)
    for step in range(steps):
        partial = partial + lax.dot_general(results[step], rows4[step], NT, preferred_element_type=jnp.float32)
    for axis in ("y", "zh", "zl"):
        partial = functools.reduce(jnp.add, line(partial, axis))
    halves = border_signs.reshape(cores, probes, -1)
    border_source = (2 * jnp.where(first, halves[0], halves[1]) - 1).astype(jnp.float32)
    border_resid = (border_source - partial).astype(jnp.bfloat16)
    own_border = lax.dot_general(border_resid, border_inverse, NT, preferred_element_type=jnp.float32)
    border_solved = in_order(own_border, swap(own_border))

    solved4 = jnp.stack(results)
    mine = jnp.where(first, solved4[:own_steps], solved4[own_steps:])
    theirs = swap(jnp.where(first, solved4[own_steps:], solved4[:own_steps]))
    solved = jnp.concatenate([jnp.where(first, mine, theirs), jnp.where(first, theirs, mine)], axis=1)
    solved = solved.transpose(1, 0, 2)

    total_probes = local_probes * lax.axis_size("x")
    node_sums = jnp.sum(jnp.square(solved.astype(jnp.float32)), axis=0)
    border_sums = jnp.sum(jnp.square(border_solved), axis=0)
    node_sums, border_sums = lax.psum((node_sums, border_sums), "x")
    return solved, border_solved, node_sums / total_probes, border_sums / total_probes


def solution(mesh):
    sizes = mesh.shape
    devices = mesh.devices.reshape(2, sizes["chain"] // 2, 4, sizes["mesh"] // 4, sizes["probe"])
    return jax.shard_map(
        shards,
        mesh=Mesh(devices, AXES),
        in_specs=(
            P("x", CHAIN, NODES),
            P("x", None),
            P(CHAIN, NODES, None),
            P(CHAIN, NODES, None, None, None),
            P(CHAIN, NODES, None),
            P(CHAIN, None, NODES),
            P(),
        ),
        out_specs=(P("x", CHAIN, NODES), P("x", None), P(CHAIN, NODES), P()),
        check_vma=False,
    )
```

```python
import functools

import jax
import jax.numpy as jnp
from jax import lax
from jax.experimental import pallas as pl
from jax.experimental.pallas import tpu as pltpu
from jax.sharding import Mesh, PartitionSpec as P

AXES = ("zl", "core", "zh", "y", "x")
CHAIN, NODES = ("zl", "core"), ("zh", "y")
NT = (((1,), (1,)), ((), ()))


def start_one_of(use_first, first, second):
    @pl.when(use_first)
    def _():
        for copy in first:
            copy.start()

    @pl.when(jnp.logical_not(use_first))
    def _():
        for copy in second:
            copy.start()


def arrange_kernel(place, *refs, per_core, steps, pieces, slices):
    own_refs, other_refs = refs[:pieces], refs[pieces : 2 * pieces]
    outs, sems = refs[-1 - steps : -1], refs[-1]

    def copies(refs, step):
        return [
            pltpu.make_async_copy(*slices(ref, k, outs[step], step % per_core), sems.at[step, k])
            for k, ref in enumerate(refs)
        ]

    waits = []
    for step in range(steps):
        own, other = copies(own_refs, step), copies(other_refs, step)
        start_one_of(place[0] == step // per_core, own, other)
        waits += own
    for copy in waits:
        copy.wait()


def factor_slices(ref, k, out, i):
    return ref.at[i], out


def finish(total, outs):
    result = total.astype(jnp.bfloat16)
    outs[0][...] = result
    if len(outs) > 1:
        for peer in range(outs[1].shape[0]):
            outs[1][peer] = result


def early_kernel(place, r_ref, own_ref, other_ref, *refs, step, per_core):
    outs, (l_buf, sems) = refs[:-2], refs[-2:]
    chunks, _, wide = l_buf.shape
    own, other = (
        [
            pltpu.make_async_copy(
                source.at[step % per_core, :, pl.ds(i * wide, wide)], l_buf.at[i], sems.at[i]
            )
            for i in range(chunks)
        ]
        for source in (own_ref, other_ref)
    )
    start_one_of(place[0] == step // per_core, own, other)
    width = r_ref.shape[2]
    per = wide // width
    total = jnp.zeros((r_ref.shape[1], l_buf.shape[1]), jnp.float32)
    for i in range(chunks):
        own[i].wait()
        left = jnp.concatenate([r_ref[i * per + j] for j in range(per)], axis=1)
        total = total + lax.dot_general(left, l_buf[i], NT, preferred_element_type=jnp.float32)
    finish(total, outs)


def early_couple_kernel(place, cols, x_ref, s_ref, own_ref, other_ref, out_ref, c_buf, sem, *, step, per_core):
    rows, slots, block, _ = c_buf.shape
    own, other = (
        [pltpu.make_async_copy(source.at[step % per_core], c_buf, sem)] for source in (own_ref, other_ref)
    )
    start_one_of(place[0] == step // per_core, own, other)
    own[0].wait()
    per = x_ref.shape[2] // block
    for row in range(rows):
        total = None
        for slot in range(slots):
            col = cols[(step * rows + row) * slots + slot]
            lanes = pl.ds(pl.multiple_of((col % per) * block, block), block)
            term = lax.dot_general(
                x_ref[col // per, :, lanes], c_buf[row, slot], NT, preferred_element_type=jnp.float32
            )
            total = term if total is None else total + term
        span = slice(row * block, (row + 1) * block)
        resid = (s_ref[:, span].astype(jnp.float32) - total).astype(jnp.bfloat16)
        for peer in range(out_ref.shape[0]):
            out_ref[peer, :, span] = resid


def apply_kernel(r_ref, l_ref, *outs):
    peers, probes, width = r_ref.shape
    group = 4

    def body(i, total):
        for j in range(group):
            lanes = pl.ds(pl.multiple_of((i * group + j) * width, width), width)
            total = total + lax.dot_general(
                r_ref[i * group + j], l_ref[:, lanes], NT, preferred_element_type=jnp.float32
            )
        return total

    start = jnp.zeros((probes, l_ref.shape[0]), jnp.float32)
    finish(lax.fori_loop(0, peers // group, body, start), outs)


VMEM = pl.BlockSpec(memory_space=pltpu.VMEM)
SMEM = pl.BlockSpec(memory_space=pltpu.SMEM)
HBM = pl.BlockSpec(memory_space=pltpu.HBM)
PARAMS = pltpu.CompilerParams(vmem_limit_bytes=16 << 20)
LARGE = pltpu.CompilerParams(vmem_limit_bytes=50 << 20)


def arrange(slices, place, own, other, steps, shape, name, after):
    pieces = len(own)
    return pl.pallas_call(
        functools.partial(
            arrange_kernel, per_core=steps // 2, steps=steps, pieces=pieces, slices=slices
        ),
        out_shape=tuple([jax.ShapeDtypeStruct(shape, jnp.bfloat16)] * steps),
        in_specs=[SMEM] + [HBM] * (2 * pieces + 1),
        out_specs=tuple([HBM] * steps),
        scratch_shapes=[pltpu.SemaphoreType.DMA((steps, pieces))],
        compiler_params=LARGE,
        cost_estimate=pl.CostEstimate(
            flops=0, transcendentals=0, bytes_accessed=4 * steps * shape[0] * shape[1]
        ),
        name=name,
    )(place, *own, *other, after)


def solved_shapes(probes, rows, peers):
    shapes = [jax.ShapeDtypeStruct((probes, rows), jnp.bfloat16)]
    if peers:
        shapes.append(jax.ShapeDtypeStruct((peers, probes, rows), jnp.bfloat16))
    return tuple(shapes)


def apply_factor(pieces, factor, spread):
    peers, probes, _ = pieces.shape
    shapes = solved_shapes(probes, factor.shape[0], peers if spread else 0)
    return pl.pallas_call(
        apply_kernel,
        out_shape=shapes,
        in_specs=[VMEM, VMEM],
        out_specs=tuple([VMEM] * len(shapes)),
        compiler_params=PARAMS,
        name="apply",
    )(pieces, factor)


def apply_early(place, pieces, own, other, step):
    peers, probes, _ = pieces.shape
    per_core, rows, width = own.shape
    shapes = solved_shapes(probes, rows, peers)
    return pl.pallas_call(
        functools.partial(early_kernel, step=step, per_core=per_core),
        out_shape=shapes,
        in_specs=[SMEM, VMEM, HBM, HBM],
        out_specs=tuple([VMEM] * len(shapes)),
        scratch_shapes=[
            pltpu.VMEM((4, rows, width // 4), own.dtype),
            pltpu.SemaphoreType.DMA((4,)),
        ],
        compiler_params=LARGE,
        name="apply_early",
    )(place, pieces, own, other)


def couple_early(place, cols, pieces, source, own, other, step):
    return pl.pallas_call(
        functools.partial(early_couple_kernel, step=step, per_core=own.shape[0]),
        out_shape=jax.ShapeDtypeStruct(pieces.shape, jnp.bfloat16),
        in_specs=[SMEM, SMEM, VMEM, VMEM, HBM, HBM],
        out_specs=VMEM,
        scratch_shapes=[pltpu.VMEM(own.shape[1:], own.dtype), pltpu.SemaphoreType.DMA],
        compiler_params=LARGE,
        name="couple_early",
    )(place, cols, pieces, source, own, other)


def line(value, axis):
    size = lax.axis_size(axis)
    moved = {
        k: lax.ppermute(value, axis, [(i, (i + k) % size) for i in range(size)])
        for k in range(1, size)
    }
    return [value] + [moved[k] for k in range(1, size)]


def swap(value):
    return lax.ppermute(value, "core", [(0, 1), (1, 0)])


def shards(
    signs, border_signs, inverse_factors, couplings, coupling_cols, border_rows, border_inverse
):
    local_probes, own_steps, local = signs.shape
    cores, turns = lax.axis_size("core"), lax.axis_size("zl")
    peers = lax.axis_size("zh") * lax.axis_size("y")
    probes = local_probes // cores
    steps = own_steps * cores
    core = lax.axis_index("core")
    first = core == 0
    place = jnp.stack([core, lax.axis_index("zh"), lax.axis_index("y")]).astype(jnp.int32)

    def in_order(own, other):
        return jnp.concatenate([jnp.where(first, own, other), jnp.where(first, other, own)], axis=0)

    source = (2 * signs - 1).astype(jnp.bfloat16).reshape(cores, probes, own_steps, local)
    source = source.transpose(0, 2, 1, 3)
    other_half = swap(jnp.where(first, source[1], source[0]))
    own_source = in_order(jnp.where(first, source[0], source[1]), other_half)
    spread = jnp.broadcast_to(own_source[0][None], (peers, probes, local))
    own_cols = in_order(coupling_cols, swap(coupling_cols)).reshape(-1)
    other_factors, other_couplings = swap(inverse_factors), swap(couplings)

    def everywhere(value):
        return lax.all_to_all(value, NODES, 0, 0)

    outs = apply_early(place, everywhere(spread), inverse_factors, other_factors, 0)
    factors = arrange(
        factor_slices, place, [inverse_factors], [other_factors], steps, inverse_factors.shape[1:], "factors", outs[0]
    )
    results = [outs[0]]
    for turn in range(turns):
        for step in range(1 if turn == 0 else 0, steps):
            if step > 0:
                pieces = everywhere(outs[1])
            resid = couple_early(
                place, own_cols, pieces, own_source[step], couplings, other_couplings, step
            )
            outs = apply_factor(everywhere(resid), factors[step], step + 1 < steps)
            results.append(outs[0])
        if turn + 1 < turns:
            moved = lax.ppermute(outs[0], "zl", [(turn, turn + 1)])
            pieces = everywhere(jnp.broadcast_to(moved[None], (peers, probes, local)))
            results = []

    rows4 = in_order(border_rows, swap(border_rows))
    partial = jnp.zeros((probes, border_rows.shape[1]), jnp.float32)
    for step in range(steps):
        partial = partial + lax.dot_general(results[step], rows4[step], NT, preferred_element_type=jnp.float32)
    for axis in ("y", "zh", "zl"):
        partial = functools.reduce(jnp.add, line(partial, axis))
    halves = border_signs.reshape(cores, probes, -1)
    border_source = (2 * jnp.where(first, halves[0], halves[1]) - 1).astype(jnp.float32)
    border_resid = (border_source - partial).astype(jnp.bfloat16)
    own_border = lax.dot_general(border_resid, border_inverse, NT, preferred_element_type=jnp.float32)
    border_solved = in_order(own_border, swap(own_border))

    solved4 = jnp.stack(results)
    mine = jnp.where(first, solved4[:own_steps], solved4[own_steps:])
    theirs = swap(jnp.where(first, solved4[own_steps:], solved4[:own_steps]))
    solved = jnp.concatenate([jnp.where(first, mine, theirs), jnp.where(first, theirs, mine)], axis=1)
    solved = solved.transpose(1, 0, 2)

    total_probes = local_probes * lax.axis_size("x")
    node_sums = jnp.sum(jnp.square(solved.astype(jnp.float32)), axis=0)
    border_sums = jnp.sum(jnp.square(border_solved), axis=0)
    node_sums, border_sums = lax.psum((node_sums, border_sums), "x")
    return solved, border_solved, node_sums / total_probes, border_sums / total_probes


def solution(mesh):
    sizes = mesh.shape
    devices = mesh.devices.reshape(2, sizes["chain"] // 2, 4, sizes["mesh"] // 4, sizes["probe"])
    return jax.shard_map(
        shards,
        mesh=Mesh(devices, AXES),
        in_specs=(
            P("x", CHAIN, NODES),
            P("x", None),
            P(CHAIN, NODES, None),
            P(CHAIN, NODES, None, None, None),
            P(CHAIN, NODES, None),
            P(CHAIN, None, NODES),
            P(),
        ),
        out_specs=(P("x", CHAIN, NODES), P("x", None), P(CHAIN, NODES), P()),
        check_vma=False,
    )
```

```python
import functools

import jax
import jax.numpy as jnp
from jax import lax
from jax.experimental import pallas as pl
from jax.experimental.pallas import tpu as pltpu
from jax.sharding import Mesh, PartitionSpec as P

AXES = ("zl", "core", "zh", "y", "x")
CHAIN, NODES = ("zl", "core"), ("zh", "y")
NT = (((1,), (1,)), ((), ()))


def start_one_of(use_first, first, second):
    @pl.when(use_first)
    def _():
        for copy in first:
            copy.start()

    @pl.when(jnp.logical_not(use_first))
    def _():
        for copy in second:
            copy.start()


def arrange_kernel(place, *refs, per_core, steps, pieces, slices):
    own_refs, other_refs = refs[:pieces], refs[pieces : 2 * pieces]
    outs, sems = refs[-1 - steps : -1], refs[-1]

    def copies(refs, step):
        return [
            pltpu.make_async_copy(*slices(ref, k, outs[step], step % per_core), sems.at[step, k])
            for k, ref in enumerate(refs)
        ]

    waits = []
    for step in range(steps):
        own, other = copies(own_refs, step), copies(other_refs, step)
        start_one_of(place[0] == step // per_core, own, other)
        waits += own
    for copy in waits:
        copy.wait()


def factor_slices(ref, k, out, i):
    return ref.at[i], out


def finish(total, outs):
    result = total.astype(jnp.bfloat16)
    outs[0][...] = result
    if len(outs) > 1:
        for peer in range(outs[1].shape[0]):
            outs[1][peer] = result


def early_kernel(place, r_ref, own_ref, other_ref, *refs, step, per_core):
    outs, (l_buf, sems) = refs[:-2], refs[-2:]
    chunks, _, wide = l_buf.shape
    own, other = (
        [
            pltpu.make_async_copy(
                source.at[step % per_core, :, pl.ds(i * wide, wide)], l_buf.at[i], sems.at[i]
            )
            for i in range(chunks)
        ]
        for source in (own_ref, other_ref)
    )
    start_one_of(place[0] == step // per_core, own, other)
    width = r_ref.shape[2]
    per = wide // width
    total = jnp.zeros((r_ref.shape[1], l_buf.shape[1]), jnp.float32)
    for i in range(chunks):
        own[i].wait()
        left = jnp.concatenate([r_ref[i * per + j] for j in range(per)], axis=1)
        total = total + lax.dot_general(left, l_buf[i], NT, preferred_element_type=jnp.float32)
    finish(total, outs)


def early_couple_kernel(place, cols, x_ref, s_ref, own_ref, other_ref, out_ref, c_buf, sem, *, step, per_core):
    rows, slots, block, _ = c_buf.shape
    own, other = (
        [pltpu.make_async_copy(source.at[step % per_core], c_buf, sem)] for source in (own_ref, other_ref)
    )
    start_one_of(place[0] == step // per_core, own, other)
    own[0].wait()
    per = x_ref.shape[2] // block
    for row in range(rows):
        total = None
        for slot in range(slots):
            col = cols[(step * rows + row) * slots + slot]
            lanes = pl.ds(pl.multiple_of((col % per) * block, block), block)
            term = lax.dot_general(
                x_ref[col // per, :, lanes], c_buf[row, slot], NT, preferred_element_type=jnp.float32
            )
            total = term if total is None else total + term
        span = slice(row * block, (row + 1) * block)
        resid = (s_ref[:, span].astype(jnp.float32) - total).astype(jnp.bfloat16)
        for peer in range(out_ref.shape[0]):
            out_ref[peer, :, span] = resid


def apply_kernel(r_ref, l_ref, *outs):
    peers, probes, width = r_ref.shape
    group = 4

    def body(i, total):
        for j in range(group):
            lanes = pl.ds(pl.multiple_of((i * group + j) * width, width), width)
            total = total + lax.dot_general(
                r_ref[i * group + j], l_ref[:, lanes], NT, preferred_element_type=jnp.float32
            )
        return total

    start = jnp.zeros((probes, l_ref.shape[0]), jnp.float32)
    finish(lax.fori_loop(0, peers // group, body, start), outs)


VMEM = pl.BlockSpec(memory_space=pltpu.VMEM)
SMEM = pl.BlockSpec(memory_space=pltpu.SMEM)
HBM = pl.BlockSpec(memory_space=pltpu.HBM)
PARAMS = pltpu.CompilerParams(vmem_limit_bytes=16 << 20)
LARGE = pltpu.CompilerParams(vmem_limit_bytes=50 << 20)


def arrange(slices, place, own, other, steps, shape, name, after):
    pieces = len(own)
    return pl.pallas_call(
        functools.partial(
            arrange_kernel, per_core=steps // 2, steps=steps, pieces=pieces, slices=slices
        ),
        out_shape=tuple([jax.ShapeDtypeStruct(shape, jnp.bfloat16)] * steps),
        in_specs=[SMEM] + [HBM] * (2 * pieces + 1),
        out_specs=tuple([VMEM] * steps),
        scratch_shapes=[pltpu.SemaphoreType.DMA((steps, pieces))],
        compiler_params=PARAMS,
        cost_estimate=pl.CostEstimate(
            flops=0, transcendentals=0, bytes_accessed=4 * steps * shape[0] * shape[1]
        ),
        name=name,
    )(place, *own, *other, after)


def solved_shapes(probes, rows, peers):
    shapes = [jax.ShapeDtypeStruct((probes, rows), jnp.bfloat16)]
    if peers:
        shapes.append(jax.ShapeDtypeStruct((peers, probes, rows), jnp.bfloat16))
    return tuple(shapes)


def apply_factor(pieces, factor, spread):
    peers, probes, _ = pieces.shape
    shapes = solved_shapes(probes, factor.shape[0], peers if spread else 0)
    return pl.pallas_call(
        apply_kernel,
        out_shape=shapes,
        in_specs=[VMEM, VMEM],
        out_specs=tuple([VMEM] * len(shapes)),
        compiler_params=PARAMS,
        name="apply",
    )(pieces, factor)


def apply_early(place, pieces, own, other, step):
    peers, probes, _ = pieces.shape
    per_core, rows, width = own.shape
    shapes = solved_shapes(probes, rows, peers)
    return pl.pallas_call(
        functools.partial(early_kernel, step=step, per_core=per_core),
        out_shape=shapes,
        in_specs=[SMEM, VMEM, HBM, HBM],
        out_specs=tuple([VMEM] * len(shapes)),
        scratch_shapes=[
            pltpu.VMEM((4, rows, width // 4), own.dtype),
            pltpu.SemaphoreType.DMA((4,)),
        ],
        compiler_params=LARGE,
        name="apply_early",
    )(place, pieces, own, other)


def couple_early(place, cols, pieces, source, own, other, step):
    return pl.pallas_call(
        functools.partial(early_couple_kernel, step=step, per_core=own.shape[0]),
        out_shape=jax.ShapeDtypeStruct(pieces.shape, jnp.bfloat16),
        in_specs=[SMEM, SMEM, VMEM, VMEM, HBM, HBM],
        out_specs=VMEM,
        scratch_shapes=[pltpu.VMEM(own.shape[1:], own.dtype), pltpu.SemaphoreType.DMA],
        compiler_params=LARGE,
        name="couple_early",
    )(place, cols, pieces, source, own, other)


def line(value, axis):
    size = lax.axis_size(axis)
    moved = {
        k: lax.ppermute(value, axis, [(i, (i + k) % size) for i in range(size)])
        for k in range(1, size)
    }
    return [value] + [moved[k] for k in range(1, size)]


def swap(value):
    return lax.ppermute(value, "core", [(0, 1), (1, 0)])


def shards(
    signs, border_signs, inverse_factors, couplings, coupling_cols, border_rows, border_inverse
):
    local_probes, own_steps, local = signs.shape
    cores, turns = lax.axis_size("core"), lax.axis_size("zl")
    peers = lax.axis_size("zh") * lax.axis_size("y")
    probes = local_probes // cores
    steps = own_steps * cores
    core = lax.axis_index("core")
    first = core == 0
    place = jnp.stack([core, lax.axis_index("zh"), lax.axis_index("y")]).astype(jnp.int32)

    def in_order(own, other):
        return jnp.concatenate([jnp.where(first, own, other), jnp.where(first, other, own)], axis=0)

    source = (2 * signs - 1).astype(jnp.bfloat16).reshape(cores, probes, own_steps, local)
    source = source.transpose(0, 2, 1, 3)
    other_half = swap(jnp.where(first, source[1], source[0]))
    own_source = in_order(jnp.where(first, source[0], source[1]), other_half)
    spread = jnp.broadcast_to(own_source[0][None], (peers, probes, local))
    own_cols = in_order(coupling_cols, swap(coupling_cols)).reshape(-1)
    own_factors, own_couplings, _ = lax.optimization_barrier((inverse_factors, couplings, spread))
    other_factors, other_couplings = swap(own_factors), swap(own_couplings)

    def everywhere(value):
        return lax.all_to_all(value, NODES, 0, 0)

    outs = apply_early(place, everywhere(spread), inverse_factors, other_factors, 0)
    factors = arrange(
        factor_slices, place, [inverse_factors], [other_factors], steps, inverse_factors.shape[1:], "factors", outs[0]
    )
    results = [outs[0]]
    for turn in range(turns):
        for step in range(1 if turn == 0 else 0, steps):
            if step > 0:
                pieces = everywhere(outs[1])
            resid = couple_early(
                place, own_cols, pieces, own_source[step], couplings, other_couplings, step
            )
            outs = apply_factor(everywhere(resid), factors[step], step + 1 < steps)
            results.append(outs[0])
        if turn + 1 < turns:
            moved = lax.ppermute(outs[0], "zl", [(turn, turn + 1)])
            pieces = everywhere(jnp.broadcast_to(moved[None], (peers, probes, local)))
            results = []

    rows4 = in_order(border_rows, swap(border_rows))
    partial = jnp.zeros((probes, border_rows.shape[1]), jnp.float32)
    for step in range(steps):
        partial = partial + lax.dot_general(results[step], rows4[step], NT, preferred_element_type=jnp.float32)
    for axis in ("y", "zh", "zl"):
        partial = functools.reduce(jnp.add, line(partial, axis))
    halves = border_signs.reshape(cores, probes, -1)
    border_source = (2 * jnp.where(first, halves[0], halves[1]) - 1).astype(jnp.float32)
    border_resid = (border_source - partial).astype(jnp.bfloat16)
    own_border = lax.dot_general(border_resid, border_inverse, NT, preferred_element_type=jnp.float32)
    border_solved = in_order(own_border, swap(own_border))

    solved4 = jnp.stack(results)
    mine = jnp.where(first, solved4[:own_steps], solved4[own_steps:])
    theirs = swap(jnp.where(first, solved4[own_steps:], solved4[:own_steps]))
    solved = jnp.concatenate([jnp.where(first, mine, theirs), jnp.where(first, theirs, mine)], axis=1)
    solved = solved.transpose(1, 0, 2)

    total_probes = local_probes * lax.axis_size("x")
    node_sums = jnp.sum(jnp.square(solved.astype(jnp.float32)), axis=0)
    border_sums = jnp.sum(jnp.square(border_solved), axis=0)
    node_sums, border_sums = lax.psum((node_sums, border_sums), "x")
    return solved, border_solved, node_sums / total_probes, border_sums / total_probes


def solution(mesh):
    sizes = mesh.shape
    devices = mesh.devices.reshape(2, sizes["chain"] // 2, 4, sizes["mesh"] // 4, sizes["probe"])
    return jax.shard_map(
        shards,
        mesh=Mesh(devices, AXES),
        in_specs=(
            P("x", CHAIN, NODES),
            P("x", None),
            P(CHAIN, NODES, None),
            P(CHAIN, NODES, None, None, None),
            P(CHAIN, NODES, None),
            P(CHAIN, None, NODES),
            P(),
        ),
        out_specs=(P("x", CHAIN, NODES), P("x", None), P(CHAIN, NODES), P()),
        check_vma=False,
    )
```

```python
import functools

import jax
import jax.numpy as jnp
from jax import lax
from jax.experimental import pallas as pl
from jax.experimental.pallas import tpu as pltpu
from jax.sharding import Mesh, PartitionSpec as P

AXES = ("zl", "core", "zh", "y", "x")
CHAIN, NODES = ("zl", "core"), ("zh", "y")
NT = (((1,), (1,)), ((), ()))


def start_one_of(use_first, first, second):
    @pl.when(use_first)
    def _():
        for copy in first:
            copy.start()

    @pl.when(jnp.logical_not(use_first))
    def _():
        for copy in second:
            copy.start()


def arrange_kernel(place, *refs, per_core, steps, pieces, slices):
    own_refs, other_refs = refs[:pieces], refs[pieces : 2 * pieces]
    outs, sems = refs[-1 - steps : -1], refs[-1]

    def copies(refs, step):
        return [
            pltpu.make_async_copy(*slices(ref, k, outs[step], step % per_core), sems.at[step, k])
            for k, ref in enumerate(refs)
        ]

    waits = []
    for step in range(steps):
        own, other = copies(own_refs, step), copies(other_refs, step)
        start_one_of(place[0] == step // per_core, own, other)
        waits += own
    for copy in waits:
        copy.wait()


def factor_slices(ref, k, out, i):
    return ref.at[i], out


def finish(total, outs):
    result = total.astype(jnp.bfloat16)
    outs[0][...] = result
    if len(outs) > 1:
        for peer in range(outs[1].shape[0]):
            outs[1][peer] = result


def early_kernel(place, r_ref, own_ref, other_ref, *refs, step, per_core):
    outs, (l_buf, sems) = refs[:-2], refs[-2:]
    chunks, _, wide = l_buf.shape
    own, other = (
        [
            pltpu.make_async_copy(
                source.at[step % per_core, :, pl.ds(i * wide, wide)], l_buf.at[i], sems.at[i]
            )
            for i in range(chunks)
        ]
        for source in (own_ref, other_ref)
    )
    start_one_of(place[0] == step // per_core, own, other)
    width = r_ref.shape[2]
    per = wide // width
    total = jnp.zeros((r_ref.shape[1], l_buf.shape[1]), jnp.float32)
    for i in range(chunks):
        own[i].wait()
        left = jnp.concatenate([r_ref[i * per + j] for j in range(per)], axis=1)
        total = total + lax.dot_general(left, l_buf[i], NT, preferred_element_type=jnp.float32)
    finish(total, outs)


def early_couple_kernel(place, cols, x_ref, s_ref, own_ref, other_ref, out_ref, c_buf, sem, *, step, per_core):
    rows, slots, block, _ = c_buf.shape
    own, other = (
        [pltpu.make_async_copy(source.at[step % per_core], c_buf, sem)] for source in (own_ref, other_ref)
    )
    start_one_of(place[0] == step // per_core, own, other)
    own[0].wait()
    per = x_ref.shape[2] // block
    for row in range(rows):
        total = None
        for slot in range(slots):
            col = cols[(step * rows + row) * slots + slot]
            lanes = pl.ds(pl.multiple_of((col % per) * block, block), block)
            term = lax.dot_general(
                x_ref[col // per, :, lanes], c_buf[row, slot], NT, preferred_element_type=jnp.float32
            )
            total = term if total is None else total + term
        span = slice(row * block, (row + 1) * block)
        resid = (s_ref[:, span].astype(jnp.float32) - total).astype(jnp.bfloat16)
        for peer in range(out_ref.shape[0]):
            out_ref[peer, :, span] = resid


def apply_kernel(r_ref, l_ref, *outs):
    peers, probes, width = r_ref.shape
    group = 4

    def body(i, total):
        for j in range(group):
            lanes = pl.ds(pl.multiple_of((i * group + j) * width, width), width)
            total = total + lax.dot_general(
                r_ref[i * group + j], l_ref[:, lanes], NT, preferred_element_type=jnp.float32
            )
        return total

    start = jnp.zeros((probes, l_ref.shape[0]), jnp.float32)
    finish(lax.fori_loop(0, peers // group, body, start), outs)


VMEM = pl.BlockSpec(memory_space=pltpu.VMEM)
SMEM = pl.BlockSpec(memory_space=pltpu.SMEM)
HBM = pl.BlockSpec(memory_space=pltpu.HBM)
PARAMS = pltpu.CompilerParams(vmem_limit_bytes=16 << 20)
LARGE = pltpu.CompilerParams(vmem_limit_bytes=50 << 20)


def arrange(slices, place, own, other, steps, shape, name, after):
    pieces = len(own)
    return pl.pallas_call(
        functools.partial(
            arrange_kernel, per_core=steps // 2, steps=steps, pieces=pieces, slices=slices
        ),
        out_shape=tuple([jax.ShapeDtypeStruct(shape, jnp.bfloat16)] * steps),
        in_specs=[SMEM] + [HBM] * (2 * pieces + 1),
        out_specs=tuple([VMEM] * steps),
        scratch_shapes=[pltpu.SemaphoreType.DMA((steps, pieces))],
        compiler_params=PARAMS,
        cost_estimate=pl.CostEstimate(
            flops=0, transcendentals=0, bytes_accessed=4 * steps * shape[0] * shape[1]
        ),
        name=name,
    )(place, *own, *other, after)


def solved_shapes(probes, rows, peers):
    shapes = [jax.ShapeDtypeStruct((probes, rows), jnp.bfloat16)]
    if peers:
        shapes.append(jax.ShapeDtypeStruct((peers, probes, rows), jnp.bfloat16))
    return tuple(shapes)


def apply_factor(pieces, factor, spread):
    peers, probes, _ = pieces.shape
    shapes = solved_shapes(probes, factor.shape[0], peers if spread else 0)
    return pl.pallas_call(
        apply_kernel,
        out_shape=shapes,
        in_specs=[VMEM, VMEM],
        out_specs=tuple([VMEM] * len(shapes)),
        compiler_params=PARAMS,
        name="apply",
    )(pieces, factor)


def apply_early(place, pieces, own, other, step):
    peers, probes, _ = pieces.shape
    per_core, rows, width = own.shape
    shapes = solved_shapes(probes, rows, peers)
    return pl.pallas_call(
        functools.partial(early_kernel, step=step, per_core=per_core),
        out_shape=shapes,
        in_specs=[SMEM, VMEM, HBM, HBM],
        out_specs=tuple([VMEM] * len(shapes)),
        scratch_shapes=[
            pltpu.VMEM((4, rows, width // 4), own.dtype),
            pltpu.SemaphoreType.DMA((4,)),
        ],
        compiler_params=LARGE,
        name="apply_early",
    )(place, pieces, own, other)


def couple_early(place, cols, pieces, source, own, other, step):
    return pl.pallas_call(
        functools.partial(early_couple_kernel, step=step, per_core=own.shape[0]),
        out_shape=jax.ShapeDtypeStruct(pieces.shape, jnp.bfloat16),
        in_specs=[SMEM, SMEM, VMEM, VMEM, HBM, HBM],
        out_specs=VMEM,
        scratch_shapes=[pltpu.VMEM(own.shape[1:], own.dtype), pltpu.SemaphoreType.DMA],
        compiler_params=LARGE,
        name="couple_early",
    )(place, cols, pieces, source, own, other)


def line(value, axis):
    size = lax.axis_size(axis)
    moved = {
        k: lax.ppermute(value, axis, [(i, (i + k) % size) for i in range(size)])
        for k in range(1, size)
    }
    return [value] + [moved[k] for k in range(1, size)]


def swap(value):
    return lax.ppermute(value, "core", [(0, 1), (1, 0)])


def shards(
    signs, border_signs, inverse_factors, couplings, coupling_cols, border_rows, border_inverse
):
    local_probes, own_steps, local = signs.shape
    cores, turns = lax.axis_size("core"), lax.axis_size("zl")
    peers = lax.axis_size("zh") * lax.axis_size("y")
    probes = local_probes // cores
    steps = own_steps * cores
    core = lax.axis_index("core")
    first = core == 0
    place = jnp.stack([core, lax.axis_index("zh"), lax.axis_index("y")]).astype(jnp.int32)

    def in_order(own, other):
        return jnp.concatenate([jnp.where(first, own, other), jnp.where(first, other, own)], axis=0)

    source = (2 * signs - 1).astype(jnp.bfloat16).reshape(cores, probes, own_steps, local)
    source = source.transpose(0, 2, 1, 3)
    other_half = swap(jnp.where(first, source[1], source[0]))
    own_source = in_order(jnp.where(first, source[0], source[1]), other_half)
    spread = jnp.broadcast_to(own_source[0][None], (peers, probes, local))
    own_cols = in_order(coupling_cols, swap(coupling_cols)).reshape(-1)
    own_factors, own_couplings, _ = lax.optimization_barrier((inverse_factors, couplings, spread))
    other_factors, other_couplings = swap(own_factors), swap(own_couplings)

    def everywhere(value):
        return lax.all_to_all(value, NODES, 0, 0)

    outs = apply_early(place, everywhere(spread), inverse_factors, other_factors, 0)
    factors = arrange(
        factor_slices, place, [inverse_factors], [other_factors], steps, inverse_factors.shape[1:], "factors", outs[0]
    )
    results = [outs[0]]
    other_rows, *outs = lax.optimization_barrier((swap(border_rows), *outs))
    for turn in range(turns):
        for step in range(1 if turn == 0 else 0, steps):
            if step > 0:
                pieces = everywhere(outs[1])
            if turn == 0 and step == 1:
                pieces, *factors = lax.optimization_barrier((pieces, *factors))
            resid = couple_early(
                place, own_cols, pieces, own_source[step], couplings, other_couplings, step
            )
            outs = apply_factor(everywhere(resid), factors[step], step + 1 < steps)
            results.append(outs[0])
        if turn + 1 < turns:
            moved = lax.ppermute(outs[0], "zl", [(turn, turn + 1)])
            pieces = everywhere(jnp.broadcast_to(moved[None], (peers, probes, local)))
            results = []

    rows4 = in_order(border_rows, other_rows)
    partial = jnp.zeros((probes, border_rows.shape[1]), jnp.float32)
    for step in range(steps):
        partial = partial + lax.dot_general(results[step], rows4[step], NT, preferred_element_type=jnp.float32)
    for axis in ("y", "zh", "zl"):
        partial = functools.reduce(jnp.add, line(partial, axis))
    halves = border_signs.reshape(cores, probes, -1)
    border_source = (2 * jnp.where(first, halves[0], halves[1]) - 1).astype(jnp.float32)
    border_resid = (border_source - partial).astype(jnp.bfloat16)
    own_border = lax.dot_general(border_resid, border_inverse, NT, preferred_element_type=jnp.float32)
    border_solved = in_order(own_border, swap(own_border))

    solved4 = jnp.stack(results)
    mine = jnp.where(first, solved4[:own_steps], solved4[own_steps:])
    theirs = swap(jnp.where(first, solved4[own_steps:], solved4[:own_steps]))
    solved = jnp.concatenate([jnp.where(first, mine, theirs), jnp.where(first, theirs, mine)], axis=1)
    solved = solved.transpose(1, 0, 2)

    total_probes = local_probes * lax.axis_size("x")
    node_sums = jnp.sum(jnp.square(solved.astype(jnp.float32)), axis=0)
    border_sums = jnp.sum(jnp.square(border_solved), axis=0)
    sums = jnp.concatenate([node_sums.reshape(-1, 128), border_sums.reshape(-1, 128)], axis=0)
    sums = functools.reduce(jnp.add, line(sums, "x")) / total_probes
    split = node_sums.size // 128
    return solved, border_solved, sums[:split].reshape(node_sums.shape), sums[split:].reshape(-1)


def solution(mesh):
    sizes = mesh.shape
    devices = mesh.devices.reshape(2, sizes["chain"] // 2, 4, sizes["mesh"] // 4, sizes["probe"])
    return jax.shard_map(
        shards,
        mesh=Mesh(devices, AXES),
        in_specs=(
            P("x", CHAIN, NODES),
            P("x", None),
            P(CHAIN, NODES, None),
            P(CHAIN, NODES, None, None, None),
            P(CHAIN, NODES, None),
            P(CHAIN, None, NODES),
            P(),
        ),
        out_specs=(P("x", CHAIN, NODES), P("x", None), P(CHAIN, NODES), P()),
        check_vma=False,
    )
```

```python
import functools

import jax
import jax.numpy as jnp
from jax import lax
from jax.experimental import pallas as pl
from jax.experimental.pallas import tpu as pltpu
from jax.sharding import Mesh, PartitionSpec as P

AXES = ("zl", "core", "zh", "y", "x")
CHAIN, NODES = ("zl", "core"), ("zh", "y")
NT = (((1,), (1,)), ((), ()))


def start_one_of(use_first, first, second):
    @pl.when(use_first)
    def _():
        for copy in first:
            copy.start()

    @pl.when(jnp.logical_not(use_first))
    def _():
        for copy in second:
            copy.start()


def finish(total, outs):
    result = total.astype(jnp.bfloat16)
    outs[0][...] = result
    if len(outs) > 1:
        for peer in range(outs[1].shape[0]):
            outs[1][peer] = result


def early_kernel(place, r_ref, own_ref, other_ref, *refs, step, per_core):
    outs, (l_buf, sems) = refs[:-2], refs[-2:]
    chunks, _, wide = l_buf.shape
    own, other = (
        [
            pltpu.make_async_copy(
                source.at[step % per_core, :, pl.ds(i * wide, wide)], l_buf.at[i], sems.at[i]
            )
            for i in range(chunks)
        ]
        for source in (own_ref, other_ref)
    )
    start_one_of(place[0] == step // per_core, own, other)
    width = r_ref.shape[2]
    per = wide // width
    total = jnp.zeros((r_ref.shape[1], l_buf.shape[1]), jnp.float32)
    for i in range(chunks):
        own[i].wait()
        left = jnp.concatenate([r_ref[i * per + j] for j in range(per)], axis=1)
        total = total + lax.dot_general(left, l_buf[i], NT, preferred_element_type=jnp.float32)
    finish(total, outs)


def couple_kernel(cols, x_ref, s_ref, c_ref, out_ref, *, step):
    rows, slots, block, _ = c_ref.shape
    per = x_ref.shape[2] // block
    for row in range(rows):
        total = None
        for slot in range(0, slots, 2):
            left = []
            for pair in range(2):
                col = cols[(step * rows + row) * slots + slot + pair]
                lanes = pl.ds(pl.multiple_of((col % per) * block, block), block)
                left.append(x_ref[col // per, :, lanes])
            term = lax.dot_general(
                jnp.concatenate(left, axis=1),
                jnp.concatenate([c_ref[row, slot], c_ref[row, slot + 1]], axis=1),
                NT,
                preferred_element_type=jnp.float32,
            )
            total = term if total is None else total + term
        span = slice(row * block, (row + 1) * block)
        resid = (s_ref[:, span].astype(jnp.float32) - total).astype(jnp.bfloat16)
        for peer in range(out_ref.shape[0]):
            out_ref[peer, :, span] = resid


def apply_kernel(r_ref, l_ref, *outs):
    peers, probes, width = r_ref.shape
    group = 4

    def body(i, total):
        for j in range(group):
            lanes = pl.ds(pl.multiple_of((i * group + j) * width, width), width)
            total = total + lax.dot_general(
                r_ref[i * group + j], l_ref[:, lanes], NT, preferred_element_type=jnp.float32
            )
        return total

    start = jnp.zeros((probes, l_ref.shape[0]), jnp.float32)
    finish(lax.fori_loop(0, peers // group, body, start), outs)


VMEM = pl.BlockSpec(memory_space=pltpu.VMEM)
SMEM = pl.BlockSpec(memory_space=pltpu.SMEM)
HBM = pl.BlockSpec(memory_space=pltpu.HBM)
PARAMS = pltpu.CompilerParams(vmem_limit_bytes=16 << 20)
LARGE = pltpu.CompilerParams(vmem_limit_bytes=50 << 20)


def solved_shapes(probes, rows, peers):
    shapes = [jax.ShapeDtypeStruct((probes, rows), jnp.bfloat16)]
    if peers:
        shapes.append(jax.ShapeDtypeStruct((peers, probes, rows), jnp.bfloat16))
    return tuple(shapes)


def apply_factor(pieces, factor, spread):
    peers, probes, _ = pieces.shape
    shapes = solved_shapes(probes, factor.shape[0], peers if spread else 0)
    return pl.pallas_call(
        apply_kernel,
        out_shape=shapes,
        in_specs=[VMEM, VMEM],
        out_specs=tuple([VMEM] * len(shapes)),
        compiler_params=PARAMS,
        name="apply",
    )(pieces, factor)


def apply_early(place, pieces, own, other, step):
    peers, probes, _ = pieces.shape
    per_core, rows, width = own.shape
    shapes = solved_shapes(probes, rows, peers)
    return pl.pallas_call(
        functools.partial(early_kernel, step=step, per_core=per_core),
        out_shape=shapes,
        in_specs=[SMEM, VMEM, HBM, HBM],
        out_specs=tuple([VMEM] * len(shapes)),
        scratch_shapes=[
            pltpu.VMEM((4, rows, width // 4), own.dtype),
            pltpu.SemaphoreType.DMA((4,)),
        ],
        compiler_params=LARGE,
        name="apply_early",
    )(place, pieces, own, other)


def couple(cols, pieces, source, c, step):
    return pl.pallas_call(
        functools.partial(couple_kernel, step=step),
        out_shape=jax.ShapeDtypeStruct(pieces.shape, jnp.bfloat16),
        in_specs=[SMEM, VMEM, VMEM, VMEM],
        out_specs=VMEM,
        compiler_params=PARAMS,
        name="couple",
    )(cols, pieces, source, c)


def line(value, axis):
    size = lax.axis_size(axis)
    moved = {
        k: lax.ppermute(value, axis, [(i, (i + k) % size) for i in range(size)])
        for k in range(1, size)
    }
    return [value] + [moved[k] for k in range(1, size)]


def swap(value):
    return lax.ppermute(value, "core", [(0, 1), (1, 0)])


def shards(
    signs, border_signs, inverse_factors, couplings, coupling_cols, border_rows, border_inverse
):
    local_probes, own_steps, local = signs.shape
    cores, turns = lax.axis_size("core"), lax.axis_size("zl")
    peers = lax.axis_size("zh") * lax.axis_size("y")
    probes = local_probes // cores
    steps = own_steps * cores
    core = lax.axis_index("core")
    first = core == 0
    place = jnp.stack([core, lax.axis_index("zh"), lax.axis_index("y")]).astype(jnp.int32)

    def in_order(own, other):
        return jnp.concatenate([jnp.where(first, own, other), jnp.where(first, other, own)], axis=0)

    source = (2 * signs - 1).astype(jnp.bfloat16).reshape(cores, probes, own_steps, local)
    source = source.transpose(0, 2, 1, 3)
    other_half = swap(jnp.where(first, source[1], source[0]))
    own_source = in_order(jnp.where(first, source[0], source[1]), other_half)
    spread = jnp.broadcast_to(own_source[0][None], (peers, probes, local))
    own_cols = in_order(coupling_cols, swap(coupling_cols)).reshape(-1)
    own_factors, own_couplings, _ = lax.optimization_barrier((inverse_factors, couplings, spread))
    other_factors, other_couplings = swap(own_factors), swap(own_couplings)

    def everywhere(value):
        return lax.all_to_all(value, NODES, 0, 0)

    outs = apply_early(place, everywhere(spread), inverse_factors, other_factors, 0)
    other_rows, *outs = lax.optimization_barrier((swap(border_rows), *outs))
    factor_pair, coupling_pair = (inverse_factors, other_factors), (couplings, other_couplings)

    def slice_of(pair, step, after):
        own, other, _ = lax.optimization_barrier((*pair, after))
        mine = first if step < own_steps else jnp.logical_not(first)
        return jnp.where(mine, own[step % own_steps], other[step % own_steps])

    results = [outs[0]]
    for turn in range(turns):
        for step in range(1 if turn == 0 else 0, steps):
            if step > 0:
                pieces = everywhere(outs[1])
            block = slice_of(coupling_pair, step, outs[0])
            resid = couple(own_cols, pieces, own_source[step], block, step)
            factor = slice_of(factor_pair, step, resid)
            outs = apply_factor(everywhere(resid), factor, step + 1 < steps)
            results.append(outs[0])
        if turn + 1 < turns:
            moved = lax.ppermute(outs[0], "zl", [(turn, turn + 1)])
            pieces = everywhere(jnp.broadcast_to(moved[None], (peers, probes, local)))
            results = []

    rows4 = in_order(border_rows, other_rows)
    partial = jnp.zeros((probes, border_rows.shape[1]), jnp.float32)
    for step in range(steps):
        partial = partial + lax.dot_general(results[step], rows4[step], NT, preferred_element_type=jnp.float32)
    for axis in ("y", "zh", "zl"):
        partial = functools.reduce(jnp.add, line(partial, axis))
    halves = border_signs.reshape(cores, probes, -1)
    border_source = (2 * jnp.where(first, halves[0], halves[1]) - 1).astype(jnp.float32)
    border_resid = (border_source - partial).astype(jnp.bfloat16)
    own_border = lax.dot_general(border_resid, border_inverse, NT, preferred_element_type=jnp.float32)
    border_solved = in_order(own_border, swap(own_border))

    solved4 = jnp.stack(results)
    mine = jnp.where(first, solved4[:own_steps], solved4[own_steps:])
    theirs = swap(jnp.where(first, solved4[own_steps:], solved4[:own_steps]))
    solved = jnp.concatenate([jnp.where(first, mine, theirs), jnp.where(first, theirs, mine)], axis=1)
    solved = solved.transpose(1, 0, 2)

    total_probes = local_probes * lax.axis_size("x")
    node_sums = jnp.sum(jnp.square(solved.astype(jnp.float32)), axis=0)
    border_sums = jnp.sum(jnp.square(border_solved), axis=0)
    sums = jnp.concatenate([node_sums.reshape(-1, 128), border_sums.reshape(-1, 128)], axis=0)
    sums = functools.reduce(jnp.add, line(sums, "x")) / total_probes
    split = node_sums.size // 128
    return solved, border_solved, sums[:split].reshape(node_sums.shape), sums[split:].reshape(-1)


def solution(mesh):
    sizes = mesh.shape
    devices = mesh.devices.reshape(2, sizes["chain"] // 2, 4, sizes["mesh"] // 4, sizes["probe"])
    return jax.shard_map(
        shards,
        mesh=Mesh(devices, AXES),
        in_specs=(
            P("x", CHAIN, NODES),
            P("x", None),
            P(CHAIN, NODES, None),
            P(CHAIN, NODES, None, None, None),
            P(CHAIN, NODES, None),
            P(CHAIN, None, NODES),
            P(),
        ),
        out_specs=(P("x", CHAIN, NODES), P("x", None), P(CHAIN, NODES), P()),
        check_vma=False,
    )
```

```python
import functools

import jax
import jax.numpy as jnp
from jax import lax
from jax.experimental import pallas as pl
from jax.experimental.pallas import tpu as pltpu
from jax.sharding import Mesh, PartitionSpec as P

AXES = ("zl", "core", "zh", "y", "x")
CHAIN, NODES = ("zl", "core"), ("zh", "y")
NT = (((1,), (1,)), ((), ()))


def start_one_of(use_first, first, second):
    @pl.when(use_first)
    def _():
        for copy in first:
            copy.start()

    @pl.when(jnp.logical_not(use_first))
    def _():
        for copy in second:
            copy.start()


def arrange_kernel(place, *refs, per_core, which, pieces, slices):
    own_refs, other_refs = refs[:pieces], refs[pieces : 2 * pieces]
    outs, sems = refs[-1 - len(which) : -1], refs[-1]

    def copies(refs, n, step):
        return [
            pltpu.make_async_copy(*slices(ref, k, outs[n], step % per_core), sems.at[n, k])
            for k, ref in enumerate(refs)
        ]

    waits = []
    for n, step in enumerate(which):
        own, other = copies(own_refs, n, step), copies(other_refs, n, step)
        start_one_of(place[0] == step // per_core, own, other)
        waits += own
    for copy in waits:
        copy.wait()


def factor_slices(ref, k, out, i):
    return ref.at[i], out


def finish(total, outs):
    result = total.astype(jnp.bfloat16)
    outs[0][...] = result
    if len(outs) > 1:
        for peer in range(outs[1].shape[0]):
            outs[1][peer] = result


def early_kernel(place, r_ref, own_ref, other_ref, *refs, step, per_core):
    outs, (l_buf, sems) = refs[:-2], refs[-2:]
    chunks, _, wide = l_buf.shape
    own, other = (
        [
            pltpu.make_async_copy(
                source.at[step % per_core, :, pl.ds(i * wide, wide)], l_buf.at[i], sems.at[i]
            )
            for i in range(chunks)
        ]
        for source in (own_ref, other_ref)
    )
    start_one_of(place[0] == step // per_core, own, other)
    width = r_ref.shape[2]
    per = wide // width
    total = jnp.zeros((r_ref.shape[1], l_buf.shape[1]), jnp.float32)
    for i in range(chunks):
        own[i].wait()
        left = jnp.concatenate([r_ref[i * per + j] for j in range(per)], axis=1)
        total = total + lax.dot_general(left, l_buf[i], NT, preferred_element_type=jnp.float32)
    finish(total, outs)


def early_couple_kernel(place, cols, x_ref, s_ref, own_ref, other_ref, out_ref, c_buf, sem, *, step, per_core):
    rows, slots, block, _ = c_buf.shape
    own, other = (
        [pltpu.make_async_copy(source.at[step % per_core], c_buf, sem)] for source in (own_ref, other_ref)
    )
    start_one_of(place[0] == step // per_core, own, other)
    own[0].wait()
    per = x_ref.shape[2] // block
    for row in range(rows):
        total = None
        for slot in range(slots):
            col = cols[(step * rows + row) * slots + slot]
            lanes = pl.ds(pl.multiple_of((col % per) * block, block), block)
            term = lax.dot_general(
                x_ref[col // per, :, lanes], c_buf[row, slot], NT, preferred_element_type=jnp.float32
            )
            total = term if total is None else total + term
        span = slice(row * block, (row + 1) * block)
        resid = (s_ref[:, span].astype(jnp.float32) - total).astype(jnp.bfloat16)
        for peer in range(out_ref.shape[0]):
            out_ref[peer, :, span] = resid


def apply_kernel(r_ref, l_ref, *outs):
    peers, probes, width = r_ref.shape
    group = 4

    def body(i, total):
        for j in range(group):
            lanes = pl.ds(pl.multiple_of((i * group + j) * width, width), width)
            total = total + lax.dot_general(
                r_ref[i * group + j], l_ref[:, lanes], NT, preferred_element_type=jnp.float32
            )
        return total

    start = jnp.zeros((probes, l_ref.shape[0]), jnp.float32)
    finish(lax.fori_loop(0, peers // group, body, start), outs)


VMEM = pl.BlockSpec(memory_space=pltpu.VMEM)
SMEM = pl.BlockSpec(memory_space=pltpu.SMEM)
HBM = pl.BlockSpec(memory_space=pltpu.HBM)
PARAMS = pltpu.CompilerParams(vmem_limit_bytes=16 << 20)
LARGE = pltpu.CompilerParams(vmem_limit_bytes=50 << 20)


def arrange(slices, place, own, other, which, per_core, shape, name, after):
    pieces = len(own)
    return pl.pallas_call(
        functools.partial(
            arrange_kernel, per_core=per_core, which=which, pieces=pieces, slices=slices
        ),
        out_shape=tuple([jax.ShapeDtypeStruct(shape, jnp.bfloat16)] * len(which)),
        in_specs=[SMEM] + [HBM] * (2 * pieces + 1),
        out_specs=tuple([VMEM] * len(which)),
        scratch_shapes=[pltpu.SemaphoreType.DMA((len(which), pieces))],
        compiler_params=PARAMS,
        cost_estimate=pl.CostEstimate(
            flops=0, transcendentals=0, bytes_accessed=8 * len(which) * shape[0] * shape[1]
        ),
        name=name,
    )(place, *own, *other, after)


def solved_shapes(probes, rows, peers):
    shapes = [jax.ShapeDtypeStruct((probes, rows), jnp.bfloat16)]
    if peers:
        shapes.append(jax.ShapeDtypeStruct((peers, probes, rows), jnp.bfloat16))
    return tuple(shapes)


def apply_factor(pieces, factor, spread):
    peers, probes, _ = pieces.shape
    shapes = solved_shapes(probes, factor.shape[0], peers if spread else 0)
    return pl.pallas_call(
        apply_kernel,
        out_shape=shapes,
        in_specs=[VMEM, VMEM],
        out_specs=tuple([VMEM] * len(shapes)),
        compiler_params=PARAMS,
        name="apply",
    )(pieces, factor)


def apply_early(place, pieces, own, other, step):
    peers, probes, _ = pieces.shape
    per_core, rows, width = own.shape
    shapes = solved_shapes(probes, rows, peers)
    return pl.pallas_call(
        functools.partial(early_kernel, step=step, per_core=per_core),
        out_shape=shapes,
        in_specs=[SMEM, VMEM, HBM, HBM],
        out_specs=tuple([VMEM] * len(shapes)),
        scratch_shapes=[
            pltpu.VMEM((4, rows, width // 4), own.dtype),
            pltpu.SemaphoreType.DMA((4,)),
        ],
        compiler_params=LARGE,
        name="apply_early",
    )(place, pieces, own, other)


def couple_early(place, cols, pieces, source, own, other, step):
    return pl.pallas_call(
        functools.partial(early_couple_kernel, step=step, per_core=own.shape[0]),
        out_shape=jax.ShapeDtypeStruct(pieces.shape, jnp.bfloat16),
        in_specs=[SMEM, SMEM, VMEM, VMEM, HBM, HBM],
        out_specs=VMEM,
        scratch_shapes=[pltpu.VMEM(own.shape[1:], own.dtype), pltpu.SemaphoreType.DMA],
        compiler_params=LARGE,
        name="couple_early",
    )(place, cols, pieces, source, own, other)


def line(value, axis):
    size = lax.axis_size(axis)
    moved = {
        k: lax.ppermute(value, axis, [(i, (i + k) % size) for i in range(size)])
        for k in range(1, size)
    }
    return [value] + [moved[k] for k in range(1, size)]


def swap(value):
    return lax.ppermute(value, "core", [(0, 1), (1, 0)])


def shards(
    signs, border_signs, inverse_factors, couplings, coupling_cols, border_rows, border_inverse
):
    local_probes, own_steps, local = signs.shape
    cores, turns = lax.axis_size("core"), lax.axis_size("zl")
    peers = lax.axis_size("zh") * lax.axis_size("y")
    probes = local_probes // cores
    steps = own_steps * cores
    core = lax.axis_index("core")
    first = core == 0
    place = jnp.stack([core, lax.axis_index("zh"), lax.axis_index("y")]).astype(jnp.int32)

    def in_order(own, other):
        return jnp.concatenate([jnp.where(first, own, other), jnp.where(first, other, own)], axis=0)

    source = (2 * signs - 1).astype(jnp.bfloat16).reshape(cores, probes, own_steps, local)
    source = source.transpose(0, 2, 1, 3)
    other_half = swap(jnp.where(first, source[1], source[0]))
    own_source = in_order(jnp.where(first, source[0], source[1]), other_half)
    spread = jnp.broadcast_to(own_source[0][None], (peers, probes, local))
    own_cols = in_order(coupling_cols, swap(coupling_cols)).reshape(-1)
    own_factors, own_couplings, _ = lax.optimization_barrier((inverse_factors, couplings, spread))
    other_factors, other_couplings = swap(own_factors), swap(own_couplings)

    def everywhere(value):
        return lax.all_to_all(value, NODES, 0, 0)

    outs = apply_early(place, everywhere(spread), inverse_factors, other_factors, 0)
    factors = {}

    def arranged(which, after):
        slices = arrange(
            factor_slices, place, [inverse_factors], [other_factors], which, own_steps, inverse_factors.shape[1:], "factors", after
        )
        factors.update(zip(which, slices))

    results = [outs[0]]
    other_rows, *outs = lax.optimization_barrier((swap(border_rows), *outs))
    for turn in range(turns):
        for step in range(1 if turn == 0 else 0, steps):
            if step > 0:
                pieces = everywhere(outs[1])
            resid = couple_early(
                place, own_cols, pieces, own_source[step], couplings, other_couplings, step
            )
            if turn == 0 and step == 1:
                own, other, _ = lax.optimization_barrier((inverse_factors, other_factors, resid))
                low = first if step < own_steps else jnp.logical_not(first)
                factor = jnp.where(low, own[step % own_steps], other[step % own_steps])
            else:
                factor = factors[step]
            outs = apply_factor(everywhere(resid), factor, step + 1 < steps)
            results.append(outs[0])
            if turn == 0 and step == 1:
                arranged(tuple(range(2, steps)), outs[0])
            if turn == 0 and step == 2:
                arranged((0, 1), outs[0])
        if turn + 1 < turns:
            moved = lax.ppermute(outs[0], "zl", [(turn, turn + 1)])
            pieces = everywhere(jnp.broadcast_to(moved[None], (peers, probes, local)))
            results = []

    rows4 = in_order(border_rows, other_rows)
    partial = jnp.zeros((probes, border_rows.shape[1]), jnp.float32)
    for step in range(steps):
        partial = partial + lax.dot_general(results[step], rows4[step], NT, preferred_element_type=jnp.float32)
    for axis in ("y", "zh", "zl"):
        partial = functools.reduce(jnp.add, line(partial, axis))
    halves = border_signs.reshape(cores, probes, -1)
    border_source = (2 * jnp.where(first, halves[0], halves[1]) - 1).astype(jnp.float32)
    border_resid = (border_source - partial).astype(jnp.bfloat16)
    own_border = lax.dot_general(border_resid, border_inverse, NT, preferred_element_type=jnp.float32)
    border_solved = in_order(own_border, swap(own_border))

    solved4 = jnp.stack(results)
    mine = jnp.where(first, solved4[:own_steps], solved4[own_steps:])
    theirs = swap(jnp.where(first, solved4[own_steps:], solved4[:own_steps]))
    solved = jnp.concatenate([jnp.where(first, mine, theirs), jnp.where(first, theirs, mine)], axis=1)
    solved = solved.transpose(1, 0, 2)

    total_probes = local_probes * lax.axis_size("x")
    node_sums = jnp.sum(jnp.square(solved.astype(jnp.float32)), axis=0)
    border_sums = jnp.sum(jnp.square(border_solved), axis=0)
    sums = jnp.concatenate([node_sums.reshape(-1, 128), border_sums.reshape(-1, 128)], axis=0)
    sums = functools.reduce(jnp.add, line(sums, "x")) / total_probes
    split = node_sums.size // 128
    return solved, border_solved, sums[:split].reshape(node_sums.shape), sums[split:].reshape(-1)


def solution(mesh):
    sizes = mesh.shape
    devices = mesh.devices.reshape(2, sizes["chain"] // 2, 4, sizes["mesh"] // 4, sizes["probe"])
    return jax.shard_map(
        shards,
        mesh=Mesh(devices, AXES),
        in_specs=(
            P("x", CHAIN, NODES),
            P("x", None),
            P(CHAIN, NODES, None),
            P(CHAIN, NODES, None, None, None),
            P(CHAIN, NODES, None),
            P(CHAIN, None, NODES),
            P(),
        ),
        out_specs=(P("x", CHAIN, NODES), P("x", None), P(CHAIN, NODES), P()),
        check_vma=False,
    )
```

```python
import functools

import jax
import jax.numpy as jnp
from jax import lax
from jax.experimental import pallas as pl
from jax.experimental.pallas import tpu as pltpu
from jax.sharding import Mesh, PartitionSpec as P

AXES = ("zl", "core", "zh", "y", "x")
CHAIN, NODES = ("zl", "core"), ("zh", "y")
NT = (((1,), (1,)), ((), ()))


def start_one_of(use_first, first, second):
    @pl.when(use_first)
    def _():
        for copy in first:
            copy.start()

    @pl.when(jnp.logical_not(use_first))
    def _():
        for copy in second:
            copy.start()


def arrange_kernel(place, *refs, per_core, steps, pieces, slices):
    own_refs, other_refs = refs[:pieces], refs[pieces : 2 * pieces]
    outs, sems = refs[-1 - steps : -1], refs[-1]

    def copies(refs, step):
        return [
            pltpu.make_async_copy(*slices(ref, k, outs[step], step % per_core), sems.at[step, k])
            for k, ref in enumerate(refs)
        ]

    waits = []
    for step in range(steps):
        own, other = copies(own_refs, step), copies(other_refs, step)
        start_one_of(place[0] == step // per_core, own, other)
        waits += own
    for copy in waits:
        copy.wait()


def factor_slices(ref, k, out, i):
    return ref.at[i], out


def finish(total, outs):
    result = total.astype(jnp.bfloat16)
    outs[0][...] = result
    if len(outs) > 1:
        for peer in range(outs[1].shape[0]):
            outs[1][peer] = result


def early_kernel(place, r_ref, own_ref, other_ref, *refs, step, per_core):
    outs, (l_buf, sems) = refs[:-2], refs[-2:]
    chunks, _, wide = l_buf.shape
    own, other = (
        [
            pltpu.make_async_copy(
                source.at[step % per_core, :, pl.ds(i * wide, wide)], l_buf.at[i], sems.at[i]
            )
            for i in range(chunks)
        ]
        for source in (own_ref, other_ref)
    )
    start_one_of(place[0] == step // per_core, own, other)
    width = r_ref.shape[2]
    per = wide // width
    total = jnp.zeros((r_ref.shape[1], l_buf.shape[1]), jnp.float32)
    for i in range(chunks):
        own[i].wait()
        left = jnp.concatenate([r_ref[i * per + j] for j in range(per)], axis=1)
        total = total + lax.dot_general(left, l_buf[i], NT, preferred_element_type=jnp.float32)
    finish(total, outs)


def couple_kernel(cols, x_ref, s_ref, c_ref, out_ref, *, step):
    rows, slots, block, _ = c_ref.shape
    per = x_ref.shape[2] // block
    for row in range(rows):
        total = None
        for slot in range(0, slots, 2):
            left = []
            for pair in range(2):
                col = cols[(step * rows + row) * slots + slot + pair]
                lanes = pl.ds(pl.multiple_of((col % per) * block, block), block)
                left.append(x_ref[col // per, :, lanes])
            term = lax.dot_general(
                jnp.concatenate(left, axis=1),
                jnp.concatenate([c_ref[row, slot], c_ref[row, slot + 1]], axis=1),
                NT,
                preferred_element_type=jnp.float32,
            )
            total = term if total is None else total + term
        span = slice(row * block, (row + 1) * block)
        resid = (s_ref[:, span].astype(jnp.float32) - total).astype(jnp.bfloat16)
        for peer in range(out_ref.shape[0]):
            out_ref[peer, :, span] = resid


def apply_kernel(r_ref, l_ref, *outs):
    peers, probes, width = r_ref.shape
    group = 4

    def body(i, total):
        for j in range(group):
            lanes = pl.ds(pl.multiple_of((i * group + j) * width, width), width)
            total = total + lax.dot_general(
                r_ref[i * group + j], l_ref[:, lanes], NT, preferred_element_type=jnp.float32
            )
        return total

    start = jnp.zeros((probes, l_ref.shape[0]), jnp.float32)
    finish(lax.fori_loop(0, peers // group, body, start), outs)


VMEM = pl.BlockSpec(memory_space=pltpu.VMEM)
SMEM = pl.BlockSpec(memory_space=pltpu.SMEM)
HBM = pl.BlockSpec(memory_space=pltpu.HBM)
PARAMS = pltpu.CompilerParams(vmem_limit_bytes=16 << 20)
LARGE = pltpu.CompilerParams(vmem_limit_bytes=50 << 20)


def arrange(slices, place, own, other, steps, shape, name, after):
    pieces = len(own)
    return pl.pallas_call(
        functools.partial(
            arrange_kernel, per_core=steps // 2, steps=steps, pieces=pieces, slices=slices
        ),
        out_shape=tuple([jax.ShapeDtypeStruct(shape, jnp.bfloat16)] * steps),
        in_specs=[SMEM] + [HBM] * (2 * pieces + 1),
        out_specs=tuple([VMEM] * steps),
        scratch_shapes=[pltpu.SemaphoreType.DMA((steps, pieces))],
        compiler_params=PARAMS,
        cost_estimate=pl.CostEstimate(
            flops=0, transcendentals=0, bytes_accessed=4 * steps * shape[0] * shape[1]
        ),
        name=name,
    )(place, *own, *other, after)


def solved_shapes(probes, rows, peers):
    shapes = [jax.ShapeDtypeStruct((probes, rows), jnp.bfloat16)]
    if peers:
        shapes.append(jax.ShapeDtypeStruct((peers, probes, rows), jnp.bfloat16))
    return tuple(shapes)


def apply_factor(pieces, factor, spread):
    peers, probes, _ = pieces.shape
    shapes = solved_shapes(probes, factor.shape[0], peers if spread else 0)
    return pl.pallas_call(
        apply_kernel,
        out_shape=shapes,
        in_specs=[VMEM, VMEM],
        out_specs=tuple([VMEM] * len(shapes)),
        compiler_params=PARAMS,
        name="apply",
    )(pieces, factor)


def apply_early(place, pieces, own, other, step):
    peers, probes, _ = pieces.shape
    per_core, rows, width = own.shape
    shapes = solved_shapes(probes, rows, peers)
    return pl.pallas_call(
        functools.partial(early_kernel, step=step, per_core=per_core),
        out_shape=shapes,
        in_specs=[SMEM, VMEM, HBM, HBM],
        out_specs=tuple([VMEM] * len(shapes)),
        scratch_shapes=[
            pltpu.VMEM((4, rows, width // 4), own.dtype),
            pltpu.SemaphoreType.DMA((4,)),
        ],
        compiler_params=LARGE,
        name="apply_early",
    )(place, pieces, own, other)


def couple(cols, pieces, source, c, step):
    return pl.pallas_call(
        functools.partial(couple_kernel, step=step),
        out_shape=jax.ShapeDtypeStruct(pieces.shape, jnp.bfloat16),
        in_specs=[SMEM, VMEM, VMEM, VMEM],
        out_specs=VMEM,
        compiler_params=PARAMS,
        name="couple",
    )(cols, pieces, source, c)


def line(value, axis):
    size = lax.axis_size(axis)
    moved = {
        k: lax.ppermute(value, axis, [(i, (i + k) % size) for i in range(size)])
        for k in range(1, size)
    }
    return [value] + [moved[k] for k in range(1, size)]


def swap(value):
    return lax.ppermute(value, "core", [(0, 1), (1, 0)])


def shards(
    signs, border_signs, inverse_factors, couplings, coupling_cols, border_rows, border_inverse
):
    local_probes, own_steps, local = signs.shape
    cores, turns = lax.axis_size("core"), lax.axis_size("zl")
    peers = lax.axis_size("zh") * lax.axis_size("y")
    probes = local_probes // cores
    steps = own_steps * cores
    core = lax.axis_index("core")
    first = core == 0
    place = jnp.stack([core, lax.axis_index("zh"), lax.axis_index("y")]).astype(jnp.int32)

    def in_order(own, other):
        return jnp.concatenate([jnp.where(first, own, other), jnp.where(first, other, own)], axis=0)

    source = (2 * signs - 1).astype(jnp.bfloat16).reshape(cores, probes, own_steps, local)
    source = source.transpose(0, 2, 1, 3)
    other_half = swap(jnp.where(first, source[1], source[0]))
    own_source = in_order(jnp.where(first, source[0], source[1]), other_half)
    spread = jnp.broadcast_to(own_source[0][None], (peers, probes, local))
    own_cols = in_order(coupling_cols, swap(coupling_cols)).reshape(-1)
    own_factors, own_couplings, _ = lax.optimization_barrier((inverse_factors, couplings, spread))
    other_factors, other_couplings = swap(own_factors), swap(own_couplings)

    def everywhere(value):
        return lax.all_to_all(value, NODES, 0, 0)

    outs = apply_early(place, everywhere(spread), inverse_factors, other_factors, 0)
    other_rows, *outs = lax.optimization_barrier((swap(border_rows), *outs))
    factor_pair, coupling_pair = (inverse_factors, other_factors), (couplings, other_couplings)

    def slice_of(pair, step, after):
        own, other, _ = lax.optimization_barrier((*pair, after))
        mine = first if step < own_steps else jnp.logical_not(first)
        return jnp.where(mine, own[step % own_steps], other[step % own_steps])

    blocks = [slice_of(coupling_pair, step, outs[0]) for step in range(steps)]
    results = [outs[0]]
    for turn in range(turns):
        for step in range(1 if turn == 0 else 0, steps):
            if step > 0:
                pieces = everywhere(outs[1])
            block = blocks[step]
            resid = couple(own_cols, pieces, own_source[step], block, step)
            if turn == 0:
                factor = slice_of(factor_pair, step, resid)
            else:
                factor = factors[step]
            outs = apply_factor(everywhere(resid), factor, step + 1 < steps)
            results.append(outs[0])
        if turn + 1 < turns:
            moved = lax.ppermute(outs[0], "zl", [(turn, turn + 1)])
            factors = arrange(
                factor_slices, place, [inverse_factors], [other_factors], steps, inverse_factors.shape[1:], "factors", moved
            )
            pieces = everywhere(jnp.broadcast_to(moved[None], (peers, probes, local)))
            results = []

    rows4 = in_order(border_rows, other_rows)
    partial = jnp.zeros((probes, border_rows.shape[1]), jnp.float32)
    for step in range(steps):
        partial = partial + lax.dot_general(results[step], rows4[step], NT, preferred_element_type=jnp.float32)
    for axis in ("y", "zh", "zl"):
        partial = functools.reduce(jnp.add, line(partial, axis))
    halves = border_signs.reshape(cores, probes, -1)
    border_source = (2 * jnp.where(first, halves[0], halves[1]) - 1).astype(jnp.float32)
    border_resid = (border_source - partial).astype(jnp.bfloat16)
    own_border = lax.dot_general(border_resid, border_inverse, NT, preferred_element_type=jnp.float32)
    border_solved = in_order(own_border, swap(own_border))

    solved4 = jnp.stack(results)
    mine = jnp.where(first, solved4[:own_steps], solved4[own_steps:])
    theirs = swap(jnp.where(first, solved4[own_steps:], solved4[:own_steps]))
    solved = jnp.concatenate([jnp.where(first, mine, theirs), jnp.where(first, theirs, mine)], axis=1)
    solved = solved.transpose(1, 0, 2)

    total_probes = local_probes * lax.axis_size("x")
    node_sums = jnp.sum(jnp.square(solved.astype(jnp.float32)), axis=0)
    border_sums = jnp.sum(jnp.square(border_solved), axis=0)
    sums = jnp.concatenate([node_sums.reshape(-1, 128), border_sums.reshape(-1, 128)], axis=0)
    sums = functools.reduce(jnp.add, line(sums, "x")) / total_probes
    split = node_sums.size // 128
    return solved, border_solved, sums[:split].reshape(node_sums.shape), sums[split:].reshape(-1)


def solution(mesh):
    sizes = mesh.shape
    devices = mesh.devices.reshape(2, sizes["chain"] // 2, 4, sizes["mesh"] // 4, sizes["probe"])
    return jax.shard_map(
        shards,
        mesh=Mesh(devices, AXES),
        in_specs=(
            P("x", CHAIN, NODES),
            P("x", None),
            P(CHAIN, NODES, None),
            P(CHAIN, NODES, None, None, None),
            P(CHAIN, NODES, None),
            P(CHAIN, None, NODES),
            P(),
        ),
        out_specs=(P("x", CHAIN, NODES), P("x", None), P(CHAIN, NODES), P()),
        check_vma=False,
    )
```

```python
import functools

import jax
import jax.numpy as jnp
from jax import lax
from jax.experimental import pallas as pl
from jax.experimental.pallas import tpu as pltpu
from jax.sharding import Mesh, PartitionSpec as P

AXES = ("zl", "core", "zh", "y", "x")
CHAIN, NODES = ("zl", "core"), ("zh", "y")
NT = (((1,), (1,)), ((), ()))


def start_one_of(use_first, first, second):
    @pl.when(use_first)
    def _():
        for copy in first:
            copy.start()

    @pl.when(jnp.logical_not(use_first))
    def _():
        for copy in second:
            copy.start()


def arrange_kernel(place, *refs, per_core, steps, pieces, slices):
    own_refs, other_refs = refs[:pieces], refs[pieces : 2 * pieces]
    outs, sems = refs[-1 - steps : -1], refs[-1]

    def copies(refs, step):
        return [
            pltpu.make_async_copy(*slices(ref, k, outs[step], step % per_core), sems.at[step, k])
            for k, ref in enumerate(refs)
        ]

    waits = []
    for step in range(steps):
        own, other = copies(own_refs, step), copies(other_refs, step)
        start_one_of(place[0] == step // per_core, own, other)
        waits += own
    for copy in waits:
        copy.wait()


def factor_slices(ref, k, out, i):
    return ref.at[i], out


def finish(total, outs):
    result = total.astype(jnp.bfloat16)
    outs[0][...] = result
    if len(outs) > 1:
        for peer in range(outs[1].shape[0]):
            outs[1][peer] = result


def early_kernel(place, r_ref, own_ref, other_ref, *refs, step, per_core):
    outs, (l_buf, sems) = refs[:-2], refs[-2:]
    chunks, _, wide = l_buf.shape
    own, other = (
        [
            pltpu.make_async_copy(
                source.at[step % per_core, :, pl.ds(i * wide, wide)], l_buf.at[i], sems.at[i]
            )
            for i in range(chunks)
        ]
        for source in (own_ref, other_ref)
    )
    start_one_of(place[0] == step // per_core, own, other)
    width = r_ref.shape[2]
    per = wide // width
    total = jnp.zeros((r_ref.shape[1], l_buf.shape[1]), jnp.float32)
    for i in range(chunks):
        own[i].wait()
        left = jnp.concatenate([r_ref[i * per + j] for j in range(per)], axis=1)
        total = total + lax.dot_general(left, l_buf[i], NT, preferred_element_type=jnp.float32)
    finish(total, outs)


def early_couple_kernel(place, cols, x_ref, s_ref, own_ref, other_ref, out_ref, c_buf, sem, *, step, per_core):
    rows, slots, block, _ = c_buf.shape
    own, other = (
        [pltpu.make_async_copy(source.at[step % per_core], c_buf, sem)] for source in (own_ref, other_ref)
    )
    start_one_of(place[0] == step // per_core, own, other)
    own[0].wait()
    per = x_ref.shape[2] // block
    for row in range(rows):
        total = None
        for slot in range(slots):
            col = cols[(step * rows + row) * slots + slot]
            lanes = pl.ds(pl.multiple_of((col % per) * block, block), block)
            term = lax.dot_general(
                x_ref[col // per, :, lanes], c_buf[row, slot], NT, preferred_element_type=jnp.float32
            )
            total = term if total is None else total + term
        span = slice(row * block, (row + 1) * block)
        resid = (s_ref[:, span].astype(jnp.float32) - total).astype(jnp.bfloat16)
        for peer in range(out_ref.shape[0]):
            out_ref[peer, :, span] = resid


def apply_kernel(r_ref, l_ref, *outs):
    peers, probes, width = r_ref.shape
    group = 4

    def body(i, total):
        for j in range(group):
            lanes = pl.ds(pl.multiple_of((i * group + j) * width, width), width)
            total = total + lax.dot_general(
                r_ref[i * group + j], l_ref[:, lanes], NT, preferred_element_type=jnp.float32
            )
        return total

    start = jnp.zeros((probes, l_ref.shape[0]), jnp.float32)
    finish(lax.fori_loop(0, peers // group, body, start), outs)


VMEM = pl.BlockSpec(memory_space=pltpu.VMEM)
SMEM = pl.BlockSpec(memory_space=pltpu.SMEM)
HBM = pl.BlockSpec(memory_space=pltpu.HBM)
PARAMS = pltpu.CompilerParams(vmem_limit_bytes=16 << 20)
LARGE = pltpu.CompilerParams(vmem_limit_bytes=50 << 20)


def arrange(slices, place, own, other, steps, shape, name, after):
    pieces = len(own)
    return pl.pallas_call(
        functools.partial(
            arrange_kernel, per_core=steps // 2, steps=steps, pieces=pieces, slices=slices
        ),
        out_shape=tuple([jax.ShapeDtypeStruct(shape, jnp.bfloat16)] * steps),
        in_specs=[SMEM] + [HBM] * (2 * pieces + 1),
        out_specs=tuple([VMEM] * steps),
        scratch_shapes=[pltpu.SemaphoreType.DMA((steps, pieces))],
        compiler_params=PARAMS,
        cost_estimate=pl.CostEstimate(
            flops=0, transcendentals=0, bytes_accessed=4 * steps * shape[0] * shape[1]
        ),
        name=name,
    )(place, *own, *other, after)


def solved_shapes(probes, rows, peers):
    shapes = [jax.ShapeDtypeStruct((probes, rows), jnp.bfloat16)]
    if peers:
        shapes.append(jax.ShapeDtypeStruct((peers, probes, rows), jnp.bfloat16))
    return tuple(shapes)


def apply_factor(pieces, factor, spread):
    peers, probes, _ = pieces.shape
    shapes = solved_shapes(probes, factor.shape[0], peers if spread else 0)
    return pl.pallas_call(
        apply_kernel,
        out_shape=shapes,
        in_specs=[VMEM, VMEM],
        out_specs=tuple([VMEM] * len(shapes)),
        compiler_params=PARAMS,
        name="apply",
    )(pieces, factor)


def apply_early(place, pieces, own, other, step):
    peers, probes, _ = pieces.shape
    per_core, rows, width = own.shape
    shapes = solved_shapes(probes, rows, peers)
    return pl.pallas_call(
        functools.partial(early_kernel, step=step, per_core=per_core),
        out_shape=shapes,
        in_specs=[SMEM, VMEM, HBM, HBM],
        out_specs=tuple([VMEM] * len(shapes)),
        scratch_shapes=[
            pltpu.VMEM((4, rows, width // 4), own.dtype),
            pltpu.SemaphoreType.DMA((4,)),
        ],
        compiler_params=LARGE,
        name="apply_early",
    )(place, pieces, own, other)


def couple_early(place, cols, pieces, source, own, other, step):
    return pl.pallas_call(
        functools.partial(early_couple_kernel, step=step, per_core=own.shape[0]),
        out_shape=jax.ShapeDtypeStruct(pieces.shape, jnp.bfloat16),
        in_specs=[SMEM, SMEM, VMEM, VMEM, HBM, HBM],
        out_specs=VMEM,
        scratch_shapes=[pltpu.VMEM(own.shape[1:], own.dtype), pltpu.SemaphoreType.DMA],
        compiler_params=LARGE,
        name="couple_early",
    )(place, cols, pieces, source, own, other)


def line(value, axis):
    size = lax.axis_size(axis)
    moved = {
        k: lax.ppermute(value, axis, [(i, (i + k) % size) for i in range(size)])
        for k in range(1, size)
    }
    return [value] + [moved[k] for k in range(1, size)]


def swap(value):
    return lax.ppermute(value, "core", [(0, 1), (1, 0)])


def shards(
    signs, border_signs, inverse_factors, couplings, coupling_cols, border_rows, border_inverse
):
    local_probes, own_steps, local = signs.shape
    cores, turns = lax.axis_size("core"), lax.axis_size("zl")
    peers = lax.axis_size("zh") * lax.axis_size("y")
    probes = local_probes // cores
    steps = own_steps * cores
    core = lax.axis_index("core")
    first = core == 0
    place = jnp.stack([core, lax.axis_index("zh"), lax.axis_index("y")]).astype(jnp.int32)

    def in_order(own, other):
        return jnp.concatenate([jnp.where(first, own, other), jnp.where(first, other, own)], axis=0)

    source = (2 * signs - 1).astype(jnp.bfloat16).reshape(cores, probes, own_steps, local)
    source = source.transpose(0, 2, 1, 3)
    other_half = swap(jnp.where(first, source[1], source[0]))
    own_source = in_order(jnp.where(first, source[0], source[1]), other_half)
    spread = jnp.broadcast_to(own_source[0][None], (peers, probes, local))
    own_cols = in_order(coupling_cols, swap(coupling_cols)).reshape(-1)
    own_factors, own_couplings, _ = lax.optimization_barrier((inverse_factors, couplings, spread))
    other_factors, other_couplings = swap(own_factors), swap(own_couplings)

    def everywhere(value):
        return lax.all_to_all(value, NODES, 0, 0)

    outs = apply_early(place, everywhere(spread), inverse_factors, other_factors, 0)
    factors = arrange(
        factor_slices, place, [inverse_factors], [other_factors], steps, inverse_factors.shape[1:], "factors", outs[0]
    )
    results = [outs[0]]
    other_rows, *outs = lax.optimization_barrier((swap(border_rows), *outs))
    for turn in range(turns):
        for step in range(1 if turn == 0 else 0, steps):
            if step > 0:
                pieces = everywhere(outs[1])
            resid = couple_early(
                place, own_cols, pieces, own_source[step], couplings, other_couplings, step
            )
            outs = apply_factor(everywhere(resid), factors[step], step + 1 < steps)
            results.append(outs[0])
        if turn + 1 < turns:
            moved = lax.ppermute(outs[0], "zl", [(turn, turn + 1)])
            pieces = everywhere(jnp.broadcast_to(moved[None], (peers, probes, local)))
            results = []

    rows4 = in_order(border_rows, other_rows)
    partial = jnp.zeros((probes, border_rows.shape[1]), jnp.float32)
    for step in range(steps):
        partial = partial + lax.dot_general(results[step], rows4[step], NT, preferred_element_type=jnp.float32)
    for axis in ("y", "zh", "zl"):
        partial = functools.reduce(jnp.add, line(partial, axis))
    halves = border_signs.reshape(cores, probes, -1)
    border_source = (2 * jnp.where(first, halves[0], halves[1]) - 1).astype(jnp.float32)
    border_resid = (border_source - partial).astype(jnp.bfloat16)
    own_border = lax.dot_general(border_resid, border_inverse, NT, preferred_element_type=jnp.float32)
    border_solved = in_order(own_border, swap(own_border))

    solved4 = jnp.stack(results)
    mine = jnp.where(first, solved4[:own_steps], solved4[own_steps:])
    theirs = swap(jnp.where(first, solved4[own_steps:], solved4[:own_steps]))
    solved = jnp.concatenate([jnp.where(first, mine, theirs), jnp.where(first, theirs, mine)], axis=1)
    solved = solved.transpose(1, 0, 2)

    total_probes = local_probes * lax.axis_size("x")
    node_sums = jnp.sum(jnp.square(solved.astype(jnp.float32)), axis=0)
    border_sums = jnp.sum(jnp.square(border_solved), axis=0)
    sums = jnp.concatenate([node_sums.reshape(-1, 128), border_sums.reshape(-1, 128)], axis=0)
    sums = functools.reduce(jnp.add, line(sums, "x")) / total_probes
    split = node_sums.size // 128
    return solved, border_solved, sums[:split].reshape(node_sums.shape), sums[split:].reshape(-1)


def solution(mesh):
    sizes = mesh.shape
    devices = mesh.devices.reshape(2, sizes["chain"] // 2, 4, sizes["mesh"] // 4, sizes["probe"])
    return jax.shard_map(
        shards,
        mesh=Mesh(devices, AXES),
        in_specs=(
            P("x", CHAIN, NODES),
            P("x", None),
            P(CHAIN, NODES, None),
            P(CHAIN, NODES, None, None, None),
            P(CHAIN, NODES, None),
            P(CHAIN, None, NODES),
            P(),
        ),
        out_specs=(P("x", CHAIN, NODES), P("x", None), P(CHAIN, NODES), P()),
        check_vma=False,
    )
```
